256 devices in a mesh: ctx: 16 (over y_lo, z), exp: 16 (over y_hi, x, core).
Axes of the slice: x: 4, y: 4 (y_hi: 2, y_lo: 2; y = y_hi * 2 + y_lo), z: 8, core: 2. Of those that a mesh axis runs over, the one named last changes fastest.
Arguments:
- queries: bfloat16 [16, 2048, 2048], P('exp', 'ctx'), may hold values from -160 to 160
- keys: bfloat16 [16, 2048, 256], P('exp', 'ctx'), may hold values from -6 to 6
- values: bfloat16 [16, 2048, 256], P('exp', 'ctx'), may hold values from -18 to 18
- segments: int32 [16, 2048], P('exp', 'ctx'), may hold values from 0 to 3, never falling along the last dimension, each value on 1 to 1024 neighbouring positions
- residual: bfloat16 [16, 2048, 2048], P('exp', 'ctx'), may hold values from -3 to 3
- out_weight: bfloat16 [2048, 2048], P('exp'), may hold values from -0.125 to 0.125
- norm_gain: float32 [2048], replicated, may hold values from 0.5 to 1.5
- expert_ids: int32 [16, 2048, 8], P('exp', 'ctx'), may hold values from 0 to 15, all different within a row; in each aligned block of 128 rows (0 to 127, 128 to 255, ..., all dimensions but the last counted through in order) at most 72 rows name the same one
- gate_weights: float32 [16, 2048, 8], P('exp', 'ctx'), may hold values from 0.05 to 0.3
- w_gate: bfloat16 [16, 2048, 768], P('exp'), may hold values from -0.125 to 0.125
- w_up: bfloat16 [16, 2048, 768], P('exp'), may hold values from -0.125 to 0.125
- w_down: bfloat16 [16, 768, 2048], P('exp'), may hold values from -0.21875 to 0.21875
Outputs:
- mixed: bfloat16 [16, 2048, 2048], P('exp', 'ctx')
The draws below stay inside these ranges and needn't reach their ends.
Inputs may be any that keep to these rules, and one draw needn't show every extreme that they name: `expert_ids`: each row names 8 different experts; among the 128 rows of one device (aligned blocks of positions) no expert is named more than 72 times. `segments`: rollout numbers never fall along a pack; a rollout spans at most 1024 positions.
All inputs are finite; a program needn't handle non-finite values.
Results may differ from the reference program's by a relative error of at most 0.01.
Values may be sent and summed in bfloat16 or wider, within the bound.
No kernel may reach another device: no remote copies, remote signals or barrier semaphores. Data moves between devices by JAX's collectives and lax.ppermute only.
A program may use at most 128 MiB of HBM per device.

```python
import math
import jax
import jax.numpy as jnp
import numpy as np
from jax import lax

D = 2048
FF = 768
HEADS = 16
KV_HEADS = 2
HEAD_DIM = 128
SEGS = 4
TOK_DEV = 128
EXPERTS = 16
TOP = 8
CAP = 72
PACKS = 16
LENGTH = 2048
TOKENS = 32768


def shared_keys(key):
    base = jax.random.normal(jax.random.fold_in(key, 101), (PACKS, LENGTH, KV_HEADS, HEAD_DIM), jnp.float32)
    base = jnp.clip(base, -6.0, 6.0)
    return base


def draw_keys(key, part):
    base = shared_keys(key)
    return base.reshape(PACKS, LENGTH, KV_HEADS * HEAD_DIM).astype(jnp.bfloat16)


def draw_queries(key, part):
    groups = HEADS // KV_HEADS
    drawn = jax.random.normal(jax.random.fold_in(key, 104), (PACKS, LENGTH, KV_HEADS, groups, HEAD_DIM), jnp.float32)
    drawn = jnp.clip(drawn, -6.0, 6.0)
    return drawn.reshape(PACKS, LENGTH, HEADS * HEAD_DIM).astype(jnp.bfloat16)


def block_scale(key, shape, pieces, low, top_value):
    loudness, own = 1.0, jax.random.fold_in(key, 6)
    for position, blocks in pieces:
        steps = jnp.exp(jax.random.uniform(jax.random.fold_in(own, position), (blocks,), jnp.float32, low / len(pieces), top_value / len(pieces)))
        loudness = loudness * jnp.repeat(steps, shape[position] // blocks).reshape([-1 if axis == position else 1 for axis in range(len(shape))])
    return loudness


def length_profile(count, total, bound, slope):
    weights = [(1 << 20) // math.isqrt(rank ** slope) + 1 for rank in range(2, count + 1)]
    rest, given = total - bound - (count - 1), [1] * (count - 1)
    while rest > 0:
        free = [i for i in range(count - 1) if given[i] < bound]
        pool, remaining = sum([weights[i] for i in free]), rest
        for i in free:
            addition = min(bound - given[i], max(1, remaining * weights[i] // pool), rest)
            given[i] = given[i] + addition
            rest = rest - addition
    return np.array([bound] + given)


def ragged_sizes(key, number_of, total, reach, slope):
    if number_of == 2:
        one = jax.random.randint(key, (), max(1, total - reach), min(reach, total - 1) + 1)
        return jnp.stack([one, total - one])
    lengths = jnp.asarray(length_profile(number_of, total, reach, slope), jnp.int32)
    couples = (number_of - 1) // 2
    donor, taker = lengths[1:1 + 2 * couples:2], lengths[2:2 + 2 * couples:2]
    room = jnp.minimum(donor - 1, reach - taker)
    passed = jax.random.randint(jax.random.fold_in(key, 1), (couples,), 0, 1 << 20) % (room + 1)
    lengths = lengths.at[1:1 + 2 * couples:2].set(donor - passed).at[2:2 + 2 * couples:2].set(taker + passed)
    return lengths[jax.random.permutation(jax.random.fold_in(key, 2), number_of)]


def shared_out(own_key, own, number, rows, amount, top, reach, lean):
    ranking = jax.random.permutation(own_key, amount)
    crowded, usual = portions_of(amount, rows * top, reach, lean, True), portions_of(amount, rows * top, reach, lean, False)
    places = jnp.arange(amount)

    def named(tallies, offset_by):
        used = int((tallies > 0).sum())
        fixed = max(1, used // 4)
        shifted = fixed + (places - fixed + offset_by * (used - fixed)) % max(1, amount - fixed)
        return jnp.zeros((amount,), jnp.int32).at[ranking[jnp.where(places < fixed, places, shifted)]].set(jnp.asarray(tallies, jnp.int32))

    tallies = jnp.where(number % 4 == 0, named(crowded, number // 4), named(usual, number - number // 4 - 1))
    mixed = jax.random.permutation(jax.random.fold_in(own, 3), amount)
    donor, receiver = mixed[0:amount // 2 * 2:2], mixed[1:amount // 2 * 2:2]
    margin = jnp.minimum(tallies[donor] - 1, reach - tallies[receiver]) // 2
    margin = jnp.where((donor == ranking[0]) | (receiver == ranking[0]) | (tallies[receiver] == 0), 0, jnp.maximum(margin, 0))
    shifted = jax.random.randint(jax.random.fold_in(own, 4), (amount // 2,), 0, 1 << 20) % (margin + 1)
    tallies = tallies.at[donor].add(-shifted).at[receiver].add(shifted)
    labels = jnp.searchsorted(jnp.cumsum(tallies), jnp.arange(rows * top), side="right").astype(jnp.int32)
    grid = labels.reshape(top, rows).T
    grid = grid[jax.random.permutation(jax.random.fold_in(own, 1), rows)]
    offset_by = jax.random.randint(jax.random.fold_in(own, 2), (rows, 1), 0, top)
    return jnp.take_along_axis(grid, (jnp.arange(top)[None, :] + offset_by) % top, axis=1)


def portions_of(amount, total, reach, lean, full):
    weights = [(1 << 20) // math.isqrt(rank ** lean) + 1 for rank in range(1, amount + 1)]
    largest = reach if full else min(reach, max(-(-total // amount), total * weights[0] // sum(weights)))
    least = 1 if total - largest >= amount - 1 else 0
    holding, rest = [largest] + [least] * (amount - 1), total - largest - least * (amount - 1)
    while rest > 0:
        free = [i for i in range(1, amount) if holding[i] < largest] or [i for i in range(1, amount) if holding[i] < reach]
        whole, remaining = sum([weights[i] for i in free]), rest
        for i in free:
            more = min(reach - holding[i], max(1, remaining * weights[i] // whole), rest)
            holding[i] = holding[i] + more
            rest = rest - more
    return np.array(holding)


def noise(key, dims, scale, bound, split=(), held_as=jnp.bfloat16):
    values = scale * jax.random.normal(key, dims, jnp.float32)
    if split:
        values = values * block_scale(key, dims, split, -0.22, 0.18)
    return jnp.clip(values, -bound, bound).astype(held_as)


def setup_inputs(seed: int = 0) -> dict:
    key_of = jax.random.split(jax.random.key(seed), 13)
    queries = draw_queries(jax.random.fold_in(key_of[12], 71), 0)
    keys = draw_keys(jax.random.fold_in(key_of[12], 71), 0)
    values = noise(key_of[2], (PACKS, LENGTH, KV_HEADS * HEAD_DIM), 3.0, 18.0, ((0, 16), (1, 16)))
    segments = jax.vmap(lambda own: jnp.searchsorted(jnp.cumsum(ragged_sizes(own, SEGS, LENGTH, LENGTH // 2, 0)), jnp.arange(LENGTH), side="right"))(jax.random.split(key_of[3], PACKS)).reshape((PACKS, LENGTH)).astype(jnp.int32)
    residual = noise(key_of[4], (PACKS, LENGTH, D), 0.5, 3.0, ((0, 16), (1, 16)))
    out_weight = noise(key_of[5], (HEADS * HEAD_DIM, D), (HEADS * HEAD_DIM) ** -0.5, 0.125, ((0, 16),))
    norm_gain = jnp.clip(1.0 + 0.1 * jax.random.normal(key_of[6], (D,), jnp.float32), 0.5, 1.5)
    expert_ids_keys = jax.random.split(jax.random.fold_in(key_of[7], 1), PACKS * LENGTH // TOK_DEV)
    expert_ids_turns = jax.random.permutation(jax.random.fold_in(key_of[7], 3), PACKS * LENGTH // TOK_DEV)
    expert_ids = jax.vmap(lambda own, number: shared_out(jax.random.fold_in(key_of[7], 2), own, number, TOK_DEV, EXPERTS, TOP, CAP, 1))(expert_ids_keys, expert_ids_turns).reshape((PACKS, LENGTH, TOP))
    gate_weights = jnp.clip(0.05 + 0.25 * jax.random.uniform(key_of[8], (PACKS, LENGTH, TOP), jnp.float32) ** block_scale(key_of[8], (PACKS, LENGTH, TOP), ((0, 16), (1, 16)), -0.2, 0.2), 0.05, 0.3)
    w_gate = noise(key_of[9], (EXPERTS, D, FF), D ** -0.5, 0.125, ((0, 16),))
    w_up = noise(key_of[10], (EXPERTS, D, FF), D ** -0.5, 0.125, ((0, 16),))
    w_down = noise(key_of[11], (EXPERTS, FF, D), FF ** -0.5, 0.21875, ((0, 16),))
    return {"queries": queries, "keys": keys, "values": values, "segments": segments, "residual": residual, "out_weight": out_weight, "norm_gain": norm_gain, "expert_ids": expert_ids, "gate_weights": gate_weights, "w_gate": w_gate, "w_up": w_up, "w_down": w_down}


masked_score = -1e+30

def attend_block(query_block, query_pos, query_seg, key_heads, value_heads, key_seg):
    block_rows = query_block.shape[0]
    groups = HEADS // KV_HEADS
    grouped = query_block.reshape(block_rows, KV_HEADS, groups, HEAD_DIM).astype(jnp.float32)
    scores = jnp.einsum('qkgd,tkd->kgqt', grouped, key_heads, precision=lax.Precision.HIGHEST) * HEAD_DIM ** (-0.5)
    key_pos = jnp.arange(LENGTH, dtype=jnp.int32)
    visible = (key_pos[None, :] <= query_pos[:, None]) & (key_seg[None, :] == query_seg[:, None])
    scores = jnp.where(visible, scores, masked_score)
    top_score = lax.optimization_barrier(jnp.max(scores, axis=-1, keepdims=True))
    weights = jnp.where(visible, jnp.exp(scores - top_score), jnp.float32(0.0))
    totals = lax.optimization_barrier(jnp.sum(weights, axis=-1))
    rounded = lax.optimization_barrier(weights.astype(jnp.bfloat16)).astype(jnp.float32)
    summed = jnp.einsum('kgqt,tkd->kgqd', rounded, value_heads, precision=lax.Precision.HIGHEST)
    summed = summed / totals[..., None]
    return summed.transpose(2, 0, 1, 3).reshape(block_rows, HEADS * HEAD_DIM).astype(jnp.bfloat16)

def attend_pack(inputs):
    pack_queries, pack_keys, pack_values, pack_segments = inputs
    key_heads = pack_keys.reshape(LENGTH, KV_HEADS, HEAD_DIM).astype(jnp.float32)
    value_heads = pack_values.reshape(LENGTH, KV_HEADS, HEAD_DIM).astype(jnp.float32)
    block_rows = 512 if LENGTH % 512 == 0 else LENGTH
    block_count = LENGTH // block_rows

    def one_block(block_index):
        first = (block_index * block_rows).astype(jnp.int32)
        query_block = lax.dynamic_slice_in_dim(pack_queries, first, block_rows, 0)
        query_seg = lax.dynamic_slice_in_dim(pack_segments, first, block_rows, 0)
        query_pos = first + jnp.arange(block_rows, dtype=jnp.int32)
        return attend_block(query_block, query_pos, query_seg, key_heads, value_heads, pack_segments)
    blocks = lax.map(one_block, jnp.arange(block_count, dtype=jnp.int32))
    return blocks.reshape(LENGTH, HEADS * HEAD_DIM)

def reference(queries, keys, values, segments, residual, out_weight, norm_gain, expert_ids, gate_weights, w_gate, w_up, w_down):
    attended = lax.map(attend_pack, (queries, keys, values, segments))
    projected = jnp.dot(attended.reshape(TOKENS, HEADS * HEAD_DIM), out_weight, preferred_element_type=jnp.float32)
    hidden = residual.reshape(TOKENS, D).astype(jnp.float32) + projected
    scale_rows = lax.rsqrt(lax.optimization_barrier(jnp.mean(hidden * hidden, axis=-1, keepdims=True)) + 1e-06)
    normed = (hidden * scale_rows * norm_gain[None, :]).astype(jnp.bfloat16)
    blocks = TOKENS // TOK_DEV
    assigned = TOK_DEV * TOP
    flat_ids = expert_ids.reshape(blocks, assigned)
    flat_gates = gate_weights.reshape(blocks, assigned)
    onehot = (flat_ids[:, :, None] == jnp.arange(EXPERTS, dtype=jnp.int32)[None, None, :]).astype(jnp.int32)
    slots = lax.optimization_barrier(jnp.sum((jnp.cumsum(onehot, axis=1) - onehot) * onehot, axis=-1))
    block_index = jnp.arange(blocks, dtype=jnp.int32)[:, None]
    token_index = block_index * TOK_DEV + jnp.arange(assigned, dtype=jnp.int32)[None, :] // TOP
    padded_norm = jnp.concatenate([normed, jnp.zeros((1, D), jnp.bfloat16)], axis=0)
    buffer_rows = blocks * CAP

    def one_expert(total, inputs):
        expert, gate_mat, up_mat, down_mat = inputs
        chosen = flat_ids == expert
        dest = jnp.where(chosen, block_index * CAP + slots, buffer_rows).astype(jnp.int32)
        source = jnp.full((buffer_rows + 1,), TOKENS, jnp.int32).at[dest.ravel()].set(token_index.ravel())[:-1]
        factor = jnp.zeros((buffer_rows + 1,), jnp.float32).at[dest.ravel()].set(flat_gates.ravel())[:-1]
        factor = jnp.where(source < TOKENS, factor, jnp.float32(0.0))
        rows = padded_norm[source]
        gate_part = jnp.dot(rows, gate_mat, preferred_element_type=jnp.float32)
        up_part = jnp.dot(rows, up_mat, preferred_element_type=jnp.float32)
        activ = (jax.nn.silu(gate_part) * up_part).astype(jnp.bfloat16)
        expert_out = jnp.dot(activ, down_mat, preferred_element_type=jnp.float32).astype(jnp.bfloat16)
        total = total.at[source].add(factor[:, None] * expert_out.astype(jnp.float32), mode='drop')
        return (total, None)
    start = jnp.zeros((TOKENS, D), jnp.float32)
    moe_sum, _ = lax.scan(one_expert, start, (jnp.arange(EXPERTS, dtype=jnp.int32), w_gate, w_up, w_down))
    mixed = (hidden + moe_sum).astype(jnp.bfloat16)
    return mixed.reshape(PACKS, LENGTH, D)
```

```python
import functools

import jax
import jax.numpy as jnp
from jax import lax
from jax.experimental import pallas as pl
from jax.experimental.pallas import tpu as pltpu
from jax.sharding import PartitionSpec as P

D = 2048
HEADS = 16
HEAD_DIM = 128
ROWS = 128
EXPERTS = 16
CAP = 72
SLOTS = EXPERTS * CAP
FF = 768
HALF = D // 2
Z = 8
SEG_ROWS = 16
PART = ROWS + SEG_ROWS
KEYS = 9 * ROWS
MASKED = -1e30
BF16 = jnp.bfloat16
F32 = jnp.float32

VM = pl.BlockSpec(memory_space=pltpu.VMEM)
SM = pl.BlockSpec(memory_space=pltpu.SMEM)


def params(mib, **kw):
    return pltpu.CompilerParams(vmem_limit_bytes=mib << 20, **kw)


def exp_pairs(f):
    pairs = []
    for e in range(16):
        y, x, c = f(e // 8, (e // 2) % 4, e % 2)
        pairs.append((e, (y % 2) * 8 + (x % 4) * 2 + c % 2))
    return pairs


CORE_SWAP = exp_pairs(lambda y, x, c: (y, x, c + 1))
Y_SWAP = exp_pairs(lambda y, x, c: (y + 1, x, c))
X_GROUPS = [[y * 8 + x * 2 + c for x in range(4)] for y in range(2) for c in range(2)]
Z_GROUPS = [list(range(8)), list(range(8, 16))]


def swap(v):
    return lax.ppermute(v, "exp", CORE_SWAP)


def y_swap(v):
    return lax.ppermute(v, "exp", Y_SWAP)


def x_spread(v):
    sent = jnp.broadcast_to(v[None], (4,) + v.shape)
    return lax.all_to_all(
        sent, "exp", split_axis=0, concat_axis=0, tiled=True, axis_index_groups=X_GROUPS
    )


def gather_weight(w):
    first, second = w[:, :HALF], w[:, HALF:]
    first_y = y_swap(first)
    second_x = x_spread(second)
    first_y, second_x = lax.optimization_barrier((first_y, second_x))
    second_y = y_swap(second_x)
    first_all = x_spread(jnp.stack([first, first_y]))
    first_other = swap(first_all)
    second_all = jnp.stack([second_x, second_y], axis=1)
    second_other = swap(second_all)
    flat = [v.reshape(8 * ROWS, HALF) for v in (first_all, first_other, second_all, second_other)]
    return flat


def attention_kernel(place, q_ref, kv_ref, qseg_ref, out_ref, kcat, bias):
    z, hi, y, c = place[0], place[1], place[2], place[3]
    qpos = (hi * Z + z) * ROWS + lax.broadcasted_iota(jnp.int32, (ROWS, ROWS), 0)
    lane = lax.broadcasted_iota(jnp.int32, (ROWS, ROWS), 1)
    qseg = qseg_ref[...]
    for j in range(9):
        if j < 8:
            upper = (z < j).astype(jnp.int32)
            at = j * (2 * PART) + (1 - upper) * PART
            first = jnp.where(
                upper == 1, jnp.where(hi == 1, j * ROWS, 1 << 20), (hi * Z + j) * ROWS
            )
        else:
            at = z * (2 * PART)
            first = jnp.where(hi == 1, z * ROWS, 1 << 20)
        at = pl.multiple_of(at, 16)
        kcat[pl.ds(j * ROWS, ROWS), :] = kv_ref[pl.ds(at, ROWS), :]
        kseg = kv_ref[pl.ds(pl.multiple_of(at + ROWS, 16), SEG_ROWS), 0:ROWS].astype(F32)[0:1, :]
        visible = (first + lane <= qpos) & (kseg == qseg)
        bias[:, pl.ds(j * ROWS, ROWS)] = jnp.where(visible, F32(0.0), F32(MASKED))
    scale = HEAD_DIM ** (-0.5)
    for rel in range(2):
        for yy in range(2):
            kvh = lax.rem(y + yy, 2)
            base = kvh * 8 + lax.rem(c + rel, 2)
            qs = jnp.concatenate(
                [
                    q_ref[:, pl.ds(pl.multiple_of((base + 2 * x) * HEAD_DIM, 128), HEAD_DIM)]
                    for x in range(4)
                ],
                axis=0,
            )
            k = kcat[:, pl.ds(pl.multiple_of(kvh * HEAD_DIM, 128), HEAD_DIM)]
            v = kcat[:, pl.ds(pl.multiple_of(256 + kvh * HEAD_DIM, 128), HEAD_DIM)]
            s = lax.dot_general(qs, k, (((1,), (1,)), ((), ())), preferred_element_type=F32)
            s = s.reshape(4, ROWS, KEYS) * scale + bias[...][None]
            top = jnp.max(s, axis=-1, keepdims=True)
            w = jnp.exp(s - top)
            total = jnp.sum(w, axis=-1, keepdims=True).reshape(4 * ROWS, 1)
            a = jnp.dot(
                w.astype(BF16).reshape(4 * ROWS, KEYS), v, preferred_element_type=F32
            )
            a = (a / total).astype(BF16)
            for x in range(4):
                out_ref[:, pl.ds(rel * HALF + (2 * x + yy) * HEAD_DIM, HEAD_DIM)] = a[
                    x * ROWS : (x + 1) * ROWS
                ]


def attention(place, q, kv, qseg):
    return pl.pallas_call(
        attention_kernel,
        out_shape=jax.ShapeDtypeStruct((ROWS, D), BF16),
        in_specs=[SM, VM, VM, VM],
        out_specs=VM,
        scratch_shapes=[pltpu.VMEM((KEYS, 512), BF16), pltpu.VMEM((ROWS, KEYS), F32)],
        compiler_params=params(40),
        cost_estimate=pl.CostEstimate(
            flops=4 * HEADS * ROWS * KEYS * HEAD_DIM,
            bytes_accessed=4 << 20,
            transcendentals=HEADS * ROWS * KEYS,
        ),
    )(place, q, kv, qseg)


def project_kernel(att_ref, fo, fx, so, sx, res_ref, gain_ref, ids_ref, hid_ref, out_ref):
    own, other = att_ref[:, :HALF], att_ref[:, HALF:]
    left = jnp.dot(own, fo[...], preferred_element_type=F32) + jnp.dot(
        other, fx[...], preferred_element_type=F32
    )
    right = jnp.dot(own, so[...], preferred_element_type=F32) + jnp.dot(
        other, sx[...], preferred_element_type=F32
    )
    left = left + res_ref[:, :HALF].astype(F32)
    right = right + res_ref[:, HALF:].astype(F32)
    hid_ref[:, :HALF] = left
    hid_ref[:, HALF:] = right
    square = jnp.sum(left * left, axis=-1, keepdims=True) + jnp.sum(
        right * right, axis=-1, keepdims=True
    )
    scale = lax.rsqrt(square * (1.0 / D) + 1e-06)
    gain = gain_ref[...]
    normed = jnp.concatenate(
        [(left * scale * gain[:, :HALF]), (right * scale * gain[:, HALF:])], axis=1
    ).astype(BF16)
    expert = lax.broadcasted_iota(jnp.int32, (EXPERTS, ROWS), 0)
    named = jnp.zeros((EXPERTS, ROWS), F32)
    for k in range(8):
        named = named + (ids_ref[k : k + 1, :] == expert).astype(F32)
    before = (
        lax.broadcasted_iota(jnp.int32, (ROWS, ROWS), 0)
        < lax.broadcasted_iota(jnp.int32, (ROWS, ROWS), 1)
    ).astype(BF16)
    rank = jnp.dot(named.astype(BF16), before, preferred_element_type=F32)
    rank = jnp.where(named > 0.5, rank, F32(-1.0)).astype(BF16)
    row = lax.broadcasted_iota(jnp.int32, (SLOTS, EXPERTS), 0)
    first = lax.broadcasted_iota(jnp.int32, (SLOTS, EXPERTS), 1) * CAP
    spread = ((row >= first) & (row < first + CAP)).astype(BF16)
    at = jnp.dot(spread, rank, preferred_element_type=F32)
    slot = lax.broadcasted_iota(jnp.int32, (SLOTS, ROWS), 0)
    slot = slot - (slot // CAP) * CAP
    pick = (at == slot.astype(F32)).astype(BF16)
    step = 2 * CAP
    for r in range(SLOTS // step):
        out_ref[pl.ds(r * step, step), :] = jnp.dot(
            pick[r * step : (r + 1) * step], normed, preferred_element_type=F32
        ).astype(BF16)


def project(att, weight, residual, gain, ids_t):
    return pl.pallas_call(
        project_kernel,
        out_shape=(
            jax.ShapeDtypeStruct((ROWS, D), F32),
            jax.ShapeDtypeStruct((SLOTS, D), BF16),
        ),
        in_specs=[VM] * 8,
        out_specs=(VM, VM),
        compiler_params=params(48),
        cost_estimate=pl.CostEstimate(
            flops=2 * ROWS * D * D + 2 * SLOTS * ROWS * D,
            bytes_accessed=15 << 20,
            transcendentals=ROWS,
        ),
    )(att, *weight, residual, gain, ids_t)


def expert_kernel(x_ref, g_ref, u_ref, d_ref, o_ref):
    x = x_ref[...]
    gate = jnp.dot(x, g_ref[...], preferred_element_type=F32)
    up = jnp.dot(x, u_ref[...], preferred_element_type=F32)
    activ = (gate / (1.0 + jnp.exp(-gate)) * up).astype(BF16)
    o_ref[...] = jnp.dot(activ, d_ref[...], preferred_element_type=F32).astype(BF16)


def experts(x, w_gate, w_up, w_down):
    tile = 384
    whole = lambda i: (0, 0)
    return pl.pallas_call(
        expert_kernel,
        grid=(SLOTS // tile,),
        out_shape=jax.ShapeDtypeStruct((SLOTS, D), BF16),
        in_specs=[
            pl.BlockSpec((tile, D), lambda i: (i, 0)),
            pl.BlockSpec((D, FF), whole, pipeline_mode=pl.Buffered(1)),
            pl.BlockSpec((D, FF), whole, pipeline_mode=pl.Buffered(1)),
            pl.BlockSpec((FF, D), whole, pipeline_mode=pl.Buffered(1)),
        ],
        out_specs=pl.BlockSpec((tile, D), lambda i: (i, 0)),
        compiler_params=params(40),
        cost_estimate=pl.CostEstimate(
            flops=6 * SLOTS * D * FF, bytes_accessed=20 << 20, transcendentals=SLOTS * FF
        ),
    )(x, w_gate, w_up, w_down)


def combine_kernel(ans_ref, hid_ref, ids_ref, gate_ref, out_ref, pick):
    @pl.when(pl.program_id(0) == 0)
    def _():
        expert = lax.broadcasted_iota(jnp.int32, (ROWS, EXPERTS), 1)
        named = jnp.zeros((ROWS, EXPERTS), F32)
        gates = jnp.zeros((ROWS, EXPERTS), F32)
        for k in range(8):
            same = ids_ref[:, k : k + 1] == expert
            named = named + same.astype(F32)
            gates = gates + jnp.where(same, gate_ref[:, k : k + 1], F32(0.0))
        before = (
            lax.broadcasted_iota(jnp.int32, (ROWS, ROWS), 1)
            < lax.broadcasted_iota(jnp.int32, (ROWS, ROWS), 0)
        ).astype(BF16)
        rank = jnp.dot(before, named.astype(BF16), preferred_element_type=F32)
        rank = jnp.where(named > 0.5, rank, F32(-1.0)).astype(BF16)
        high = gates.astype(BF16)
        low = (gates - high.astype(F32)).astype(BF16)
        column = lax.broadcasted_iota(jnp.int32, (EXPERTS, SLOTS), 1)
        first = lax.broadcasted_iota(jnp.int32, (EXPERTS, SLOTS), 0) * CAP
        spread = ((column >= first) & (column < first + CAP)).astype(BF16)
        at = jnp.dot(rank, spread, preferred_element_type=F32)
        slot = lax.broadcasted_iota(jnp.int32, (ROWS, SLOTS), 1)
        slot = slot - (slot // CAP) * CAP
        here = at == slot.astype(F32)
        high = jnp.dot(high, spread, preferred_element_type=F32)
        low = jnp.dot(low, spread, preferred_element_type=F32)
        pick[pl.ds(0, ROWS), :] = jnp.where(here, high, F32(0.0)).astype(BF16)
        pick[pl.ds(ROWS, ROWS), :] = jnp.where(here, low, F32(0.0)).astype(BF16)

    both = jnp.dot(pick[...], ans_ref[...], preferred_element_type=F32)
    out_ref[...] = (hid_ref[...] + (both[:ROWS] + both[ROWS:])).astype(BF16)


def combine(answers, hidden, ids, gates):
    tile = 512
    return pl.pallas_call(
        combine_kernel,
        grid=(D // tile,),
        out_shape=jax.ShapeDtypeStruct((ROWS, D), BF16),
        in_specs=[
            pl.BlockSpec((SLOTS, tile), lambda i: (0, i)),
            pl.BlockSpec((ROWS, tile), lambda i: (0, i)),
            pl.BlockSpec((ROWS, 8), lambda i: (0, 0)),
            pl.BlockSpec((ROWS, 8), lambda i: (0, 0)),
        ],
        out_specs=pl.BlockSpec((ROWS, tile), lambda i: (0, i)),
        scratch_shapes=[pltpu.VMEM((2 * ROWS, SLOTS), BF16)],
        compiler_params=params(32),
        cost_estimate=pl.CostEstimate(
            flops=4 * ROWS * SLOTS * D, bytes_accessed=7 << 20, transcendentals=0
        ),
    )(answers, hidden, ids, gates)


def exchange(rows):
    sent = rows.reshape(EXPERTS, CAP, D)
    return lax.all_to_all(sent, "exp", split_axis=0, concat_axis=0, tiled=True).reshape(SLOTS, D)


def per_device(
    queries,
    keys,
    values,
    segments,
    residual,
    out_weight,
    norm_gain,
    expert_ids,
    gate_weights,
    w_gate,
    w_up,
    w_down,
):
    ctx, exp = lax.axis_index("ctx"), lax.axis_index("exp")
    place = jnp.stack([ctx % Z, ctx // Z, exp // 8, exp % 2]).astype(jnp.int32)
    seg_rows = jnp.broadcast_to(
        jnp.pad(segments.astype(BF16), ((0, 0), (0, 512 - ROWS))), (SEG_ROWS, 512)
    )
    own = jnp.concatenate(
        [jnp.concatenate([keys[0], values[0]], axis=1), seg_rows], axis=0
    )
    upper = lax.ppermute(own, "ctx", [(s, s + Z) for s in range(Z)])
    kv = lax.all_gather(
        jnp.concatenate([upper, own], axis=0),
        "ctx",
        axis=0,
        tiled=True,
        axis_index_groups=Z_GROUPS,
    )
    weight = gather_weight(out_weight)
    att = attention(place, queries[0], kv, segments[0].astype(F32)[:, None])
    ids = expert_ids[0]
    hidden, outgoing = project(att, weight, residual[0], norm_gain[None, :], ids.T)
    arrived = exchange(outgoing)
    answers = exchange(experts(arrived, w_gate[0], w_up[0], w_down[0]))
    mixed = combine(answers, hidden, ids, gate_weights[0])
    return mixed[None]


def solution(mesh):
    return jax.shard_map(
        per_device,
        mesh=mesh,
        in_specs=(
            P("exp", "ctx", None),
            P("exp", "ctx", None),
            P("exp", "ctx", None),
            P("exp", "ctx"),
            P("exp", "ctx", None),
            P("exp", None),
            P(),
            P("exp", "ctx", None),
            P("exp", "ctx", None),
            P("exp", None, None),
            P("exp", None, None),
            P("exp", None, None),
        ),
        out_specs=P("exp", "ctx", None),
        check_vma=False,
    )
```

```python
import functools

import jax
import jax.numpy as jnp
from jax import lax
from jax.experimental import pallas as pl
from jax.experimental.pallas import tpu as pltpu
from jax.sharding import PartitionSpec as P

D = 2048
HEADS = 16
HEAD_DIM = 128
ROWS = 128
EXPERTS = 16
CAP = 72
SLOTS = EXPERTS * CAP
FF = 768
HALF = D // 2
Z = 8
SEG_ROWS = 16
PART = ROWS + SEG_ROWS
KEYS = 9 * ROWS
MASKED = -1e30
BF16 = jnp.bfloat16
F32 = jnp.float32

VM = pl.BlockSpec(memory_space=pltpu.VMEM)
SM = pl.BlockSpec(memory_space=pltpu.SMEM)


def params(mib, **kw):
    return pltpu.CompilerParams(vmem_limit_bytes=mib << 20, **kw)


def exp_pairs(f):
    pairs = []
    for e in range(16):
        y, x, c = f(e // 8, (e // 2) % 4, e % 2)
        pairs.append((e, (y % 2) * 8 + (x % 4) * 2 + c % 2))
    return pairs


CORE_SWAP = exp_pairs(lambda y, x, c: (y, x, c + 1))
Y_SWAP = exp_pairs(lambda y, x, c: (y + 1, x, c))
X_GROUPS = [[y * 8 + x * 2 + c for x in range(4)] for y in range(2) for c in range(2)]
Z_GROUPS = [list(range(8)), list(range(8, 16))]


def swap(v):
    return lax.ppermute(v, "exp", CORE_SWAP)


def y_swap(v):
    return lax.ppermute(v, "exp", Y_SWAP)


def x_exchange(v):
    return lax.all_to_all(
        v, "exp", split_axis=0, concat_axis=0, tiled=True, axis_index_groups=X_GROUPS
    )


def x_spread(v):
    return x_exchange(jnp.broadcast_to(v[None], (4,) + v.shape))


def gather_weight(w, extra):
    first = jnp.concatenate([w[:, :HALF], extra], axis=0)
    second = w[:, HALF:]
    first_y = y_swap(first)
    second_x = x_spread(second)
    first_y, second_x = lax.optimization_barrier((first_y, second_x))
    second_y = y_swap(second_x)
    first_all = x_spread(jnp.stack([first, first_y]))
    own = (first_all, second_x, second_y)
    return own, tuple(swap(v) for v in own)


def gate_rows(ids, gates):
    same = ids[None, :, :] == jnp.arange(EXPERTS, dtype=jnp.int32)[:, None, None]
    table = jnp.sum(jnp.where(same, gates[None], 0.0), axis=2)
    high = table.astype(BF16)
    low = (table - high.astype(F32)).astype(BF16)
    flat = jnp.concatenate([high.reshape(2, HALF), low.reshape(2, HALF)], axis=0)
    return jnp.pad(flat, ((0, 4), (0, 0)))


def own_gates(rows, expert):
    at = (expert % 8) * ROWS
    high = lax.dynamic_slice(rows, (0, 0, ROWS + expert // 8, at), (4, 2, 1, ROWS))
    low = lax.dynamic_slice(rows, (0, 0, ROWS + 2 + expert // 8, at), (4, 2, 1, ROWS))
    return (high.astype(F32) + low.astype(F32)).reshape(8, ROWS)


def attention_kernel(place, q_ref, kv_ref, qseg_ref, out_ref, kcat, bias):
    z, hi, y, c = place[0], place[1], place[2], place[3]
    qpos = (hi * Z + z) * ROWS + lax.broadcasted_iota(jnp.int32, (ROWS, ROWS), 0)
    lane = lax.broadcasted_iota(jnp.int32, (ROWS, ROWS), 1)
    qseg = qseg_ref[...]
    for j in range(9):
        if j < 8:
            upper = (z < j).astype(jnp.int32)
            at = j * (2 * PART) + (1 - upper) * PART
            first = jnp.where(
                upper == 1, jnp.where(hi == 1, j * ROWS, 1 << 20), (hi * Z + j) * ROWS
            )
        else:
            at = z * (2 * PART)
            first = jnp.where(hi == 1, z * ROWS, 1 << 20)
        at = pl.multiple_of(at, 16)
        kcat[pl.ds(j * ROWS, ROWS), :] = kv_ref[pl.ds(at, ROWS), :]
        kseg = kv_ref[pl.ds(pl.multiple_of(at + ROWS, 16), SEG_ROWS), 0:ROWS].astype(F32)[0:1, :]
        visible = (first + lane <= qpos) & (kseg == qseg)
        bias[:, pl.ds(j * ROWS, ROWS)] = jnp.where(visible, F32(0.0), F32(MASKED))
    scale = HEAD_DIM ** (-0.5)
    for rel in range(2):
        for yy in range(2):
            kvh = lax.rem(y + yy, 2)
            base = kvh * 8 + lax.rem(c + rel, 2)
            qs = jnp.concatenate(
                [
                    q_ref[:, pl.ds(pl.multiple_of((base + 2 * x) * HEAD_DIM, 128), HEAD_DIM)]
                    for x in range(4)
                ],
                axis=0,
            )
            k = kcat[:, pl.ds(pl.multiple_of(kvh * HEAD_DIM, 128), HEAD_DIM)]
            v = kcat[:, pl.ds(pl.multiple_of(256 + kvh * HEAD_DIM, 128), HEAD_DIM)]
            s = lax.dot_general(qs, k, (((1,), (1,)), ((), ())), preferred_element_type=F32)
            s = s.reshape(4, ROWS, KEYS) * scale + bias[...][None]
            top = jnp.max(s, axis=-1, keepdims=True)
            w = jnp.exp(s - top)
            total = jnp.sum(w, axis=-1, keepdims=True).reshape(4 * ROWS, 1)
            a = jnp.dot(
                w.astype(BF16).reshape(4 * ROWS, KEYS), v, preferred_element_type=F32
            )
            a = (a / total).astype(BF16)
            for x in range(4):
                out_ref[:, pl.ds(rel * HALF + (2 * x + yy) * HEAD_DIM, HEAD_DIM)] = a[
                    x * ROWS : (x + 1) * ROWS
                ]


def attention(place, q, kv, qseg):
    return pl.pallas_call(
        attention_kernel,
        out_shape=jax.ShapeDtypeStruct((ROWS, D), BF16),
        in_specs=[SM, VM, VM, VM],
        out_specs=VM,
        scratch_shapes=[pltpu.VMEM((KEYS, 512), BF16), pltpu.VMEM((ROWS, KEYS), F32)],
        compiler_params=params(24),
        cost_estimate=pl.CostEstimate(
            flops=4 * HEADS * ROWS * KEYS * HEAD_DIM,
            bytes_accessed=4 << 20,
            transcendentals=HEADS * ROWS * KEYS,
        ),
    )(place, q, kv, qseg)


def right_rows(x_ref, y_ref):
    parts = []
    for x in range(4):
        parts += [x_ref[x], y_ref[x]]
    return jnp.concatenate(parts, axis=0)


def project_kernel(
    att_ref, fo, sox, soy, fx, sxx, sxy, res_ref, gain_ref, hid_ref, first_ref, second_ref
):
    own, other = att_ref[:, :HALF], att_ref[:, HALF:]
    fo_rows = fo[:, :, 0:ROWS, :].reshape(HALF, HALF)
    fx_rows = fx[:, :, 0:ROWS, :].reshape(HALF, HALF)
    left = jnp.dot(own, fo_rows, preferred_element_type=F32) + jnp.dot(
        other, fx_rows, preferred_element_type=F32
    )
    right = jnp.dot(own, right_rows(sox, soy), preferred_element_type=F32) + jnp.dot(
        other, right_rows(sxx, sxy), preferred_element_type=F32
    )
    left = left + res_ref[:, :HALF].astype(F32)
    right = right + res_ref[:, HALF:].astype(F32)
    hid_ref[:, :HALF] = left
    hid_ref[:, HALF:] = right
    square = jnp.sum(left * left, axis=-1, keepdims=True) + jnp.sum(
        right * right, axis=-1, keepdims=True
    )
    scale = lax.rsqrt(square * (1.0 / D) + 1e-06)
    gain = gain_ref[...]
    first_ref[...] = (left * scale * gain[:, :HALF]).astype(BF16)
    second = (right * scale * gain[:, HALF:]).astype(BF16)
    for x in range(4):
        second_ref[x] = second


def project(att, own, other, residual, gain):
    return pl.pallas_call(
        project_kernel,
        out_shape=(
            jax.ShapeDtypeStruct((ROWS, D), F32),
            jax.ShapeDtypeStruct((ROWS, HALF), BF16),
            jax.ShapeDtypeStruct((4, ROWS, HALF), BF16),
        ),
        in_specs=[VM] * 9,
        out_specs=(VM, VM, VM),
        compiler_params=params(24),
        cost_estimate=pl.CostEstimate(
            flops=2 * ROWS * D * D, bytes_accessed=11 << 20, transcendentals=ROWS
        ),
    )(att, *own, *other, residual, gain)


def pick_rows(gates):
    named = (gates > 0.0).astype(F32)
    before = (
        lax.broadcasted_iota(jnp.int32, (ROWS, ROWS), 0)
        < lax.broadcasted_iota(jnp.int32, (ROWS, ROWS), 1)
    ).astype(BF16)
    rank = jnp.dot(named.astype(BF16), before, preferred_element_type=F32)
    rank = jnp.where(named > 0.5, rank, F32(-1.0))
    row = lax.broadcasted_iota(jnp.int32, (2 * CAP, 2 * ROWS), 0)
    lane = lax.broadcasted_iota(jnp.int32, (2 * CAP, 2 * ROWS), 1)
    second = row >= CAP
    slot = jnp.where(second, row - CAP, row)
    slot = jnp.where(second == (lane >= ROWS), slot, -2).astype(F32)
    picks, scales = [], []
    for x in range(4):
        both = jnp.concatenate([rank[2 * x : 2 * x + 1], rank[2 * x + 1 : 2 * x + 2]], axis=1)
        here = (both == slot).astype(F32)
        gate = jnp.concatenate([gates[2 * x : 2 * x + 1], gates[2 * x + 1 : 2 * x + 2]], axis=1)
        scales.append(jnp.sum(here * gate, axis=1, keepdims=True))
        picks.append(here.astype(BF16))
    return picks, scales


def activate(picks, a_ref, bx_ref, by_ref, g_ref, u_ref, rows):
    for x in range(4):
        left = jnp.dot(picks[x], a_ref[x].reshape(2 * ROWS, HALF), preferred_element_type=F32)
        tokens = jnp.concatenate([bx_ref[x], by_ref[x]], axis=0)
        right = jnp.dot(picks[x], tokens, preferred_element_type=F32)
        rows[pl.ds(x * 2 * CAP, 2 * CAP), :HALF] = left.astype(BF16)
        rows[pl.ds(x * 2 * CAP, 2 * CAP), HALF:] = right.astype(BF16)
    gate = jnp.dot(rows[...], g_ref[...], preferred_element_type=F32)
    up = jnp.dot(rows[...], u_ref[...], preferred_element_type=F32)
    return (gate / (1.0 + jnp.exp(-gate)) * up).astype(BF16)


def gated_blocks(x, picks, scales, activ, d_ref):
    o = jnp.dot(activ[x * 2 * CAP : (x + 1) * 2 * CAP], d_ref[...], preferred_element_type=F32)
    o = (o * scales[x]).astype(BF16)
    return lax.dot_general(picks[x], o, (((0,), (0,)), ((), ())), preferred_element_type=F32)


def other_kernel(a_ref, bx_ref, by_ref, gate_ref, g_ref, u_ref, d_ref, out_ref, rows):
    picks, scales = pick_rows(gate_ref[...])
    activ = activate(picks, a_ref, bx_ref, by_ref, g_ref, u_ref, rows)
    for x in range(4):
        dense = gated_blocks(x, picks, scales, activ, d_ref).astype(BF16)
        for yy in range(2):
            out_ref[0, x, yy] = dense[yy * ROWS : (yy + 1) * ROWS, :HALF]
            out_ref[1, x, yy] = dense[yy * ROWS : (yy + 1) * ROWS, HALF:]


def own_up_kernel(a_ref, bx_ref, by_ref, gate_ref, g_ref, u_ref, out_ref, rows):
    picks, _ = pick_rows(gate_ref[...])
    out_ref[...] = activate(picks, a_ref, bx_ref, by_ref, g_ref, u_ref, rows)


def own_down_kernel(activ_ref, gate_ref, d_ref, add_ref, keep_ref, send_ref, both_ref):
    picks, scales = pick_rows(gate_ref[...])
    activ = activ_ref[...]
    for x in range(4):
        dense = gated_blocks(x, picks, scales, activ, d_ref)
        for yy in range(2):
            d = dense[yy * ROWS : (yy + 1) * ROWS]
            part = (d[:, :HALF] + add_ref[0, x, yy].astype(F32)).astype(BF16)
            (send_ref if yy else keep_ref)[x] = part
            both_ref[x, yy] = (d[:, HALF:] + add_ref[1, x, yy].astype(F32)).astype(BF16)


PICKED = SLOTS // 2
ROW_SCRATCH = pltpu.VMEM((PICKED, D), BF16)


def kernel_call(body, out_shape, mib, flops, moved, scratch=()):
    many = isinstance(out_shape, tuple)

    def call(*operands):
        return pl.pallas_call(
            body,
            out_shape=out_shape,
            in_specs=[VM] * len(operands),
            out_specs=(VM,) * len(out_shape) if many else VM,
            scratch_shapes=scratch,
            compiler_params=params(mib),
            cost_estimate=pl.CostEstimate(flops=flops, bytes_accessed=moved, transcendentals=0),
        )(*operands)

    return call


def shape(*dims, dtype=BF16):
    return jax.ShapeDtypeStruct(dims, dtype)


def experts_other(tokens, gates, w_gate, w_up, w_down):
    return kernel_call(
        other_kernel,
        shape(2, 4, 2, ROWS, HALF),
        30,
        6 * PICKED * D * FF,
        16 << 20,
        [ROW_SCRATCH],
    )(*tokens, gates, w_gate, w_up, w_down)


def experts_own_up(tokens, gates, w_gate, w_up):
    return kernel_call(
        own_up_kernel, shape(PICKED, FF), 24, 4 * PICKED * D * FF, 10 << 20, [ROW_SCRATCH]
    )(*tokens, gates, w_gate, w_up)


def experts_own_down(activ, gates, w_down, add):
    return kernel_call(
        own_down_kernel,
        (shape(4, ROWS, HALF), shape(4, ROWS, HALF), shape(4, 2, ROWS, HALF)),
        24,
        2 * PICKED * D * FF,
        12 << 20,
    )(activ, gates, w_down, add)


def final_kernel(hid_ref, x_ref, b_ref, y_ref, out_ref):
    left = hid_ref[:, :HALF]
    for x in range(4):
        left = left + x_ref[x].astype(F32)
    out_ref[:, :HALF] = left.astype(BF16)
    right = hid_ref[:, HALF:] + (b_ref[...] + y_ref[...].astype(F32))
    out_ref[:, HALF:] = right.astype(BF16)


def spread_tokens(first, second):
    first_y = y_swap(first)
    second_x = x_exchange(second)
    first_y, second_x = lax.optimization_barrier((first_y, second_x))
    second_y = y_swap(second_x)
    first_all = x_spread(jnp.stack([first, first_y]))
    own = (first_all, second_x, second_y)
    return own, tuple(swap(v) for v in own)


def reduce_back(keep, send, both, hidden):
    got_y = y_swap(send)
    got_x = x_exchange(both)
    part_a = (keep.astype(F32) + got_y.astype(F32)).astype(BF16)
    part_b = jnp.sum(got_x.astype(F32), axis=0)
    last_y = y_swap(part_b[1].astype(BF16))
    last_x = x_exchange(part_a)
    return kernel_call(final_kernel, shape(ROWS, D), 12, ROWS * D, 4 << 20)(
        hidden, last_x, part_b[0], last_y
    )


def per_device(
    queries,
    keys,
    values,
    segments,
    residual,
    out_weight,
    norm_gain,
    expert_ids,
    gate_weights,
    w_gate,
    w_up,
    w_down,
):
    ctx, exp = lax.axis_index("ctx"), lax.axis_index("exp")
    place = jnp.stack([ctx % Z, ctx // Z, exp // 8, exp % 2]).astype(jnp.int32)
    seg_rows = jnp.broadcast_to(
        jnp.pad(segments.astype(BF16), ((0, 0), (0, 512 - ROWS))), (SEG_ROWS, 512)
    )
    own = jnp.concatenate(
        [jnp.concatenate([keys[0], values[0]], axis=1), seg_rows], axis=0
    )
    upper = lax.ppermute(own, "ctx", [(s, s + Z) for s in range(Z)])
    kv = lax.all_gather(
        jnp.concatenate([upper, own], axis=0),
        "ctx",
        axis=0,
        tiled=True,
        axis_index_groups=Z_GROUPS,
    )
    weight, weight_other = gather_weight(
        out_weight, gate_rows(expert_ids[0], gate_weights[0])
    )
    att = attention(place, queries[0], kv, segments[0].astype(F32)[:, None])
    hidden, first, second = project(att, weight, weight_other, residual[0], norm_gain[None, :])
    own, other = spread_tokens(first, second)
    gates, gates_other = own_gates(weight[0], exp), own_gates(weight_other[0], exp)
    partial = swap(experts_other(other, gates_other, w_gate[0], w_up[0], w_down[0]))
    activ = experts_own_up(own, gates, w_gate[0], w_up[0])
    keep, send, both = experts_own_down(activ, gates, w_down[0], partial)
    return reduce_back(keep, send, both, hidden)[None]


def solution(mesh):
    return jax.shard_map(
        per_device,
        mesh=mesh,
        in_specs=(
            P("exp", "ctx", None),
            P("exp", "ctx", None),
            P("exp", "ctx", None),
            P("exp", "ctx"),
            P("exp", "ctx", None),
            P("exp", None),
            P(),
            P("exp", "ctx", None),
            P("exp", "ctx", None),
            P("exp", None, None),
            P("exp", None, None),
            P("exp", None, None),
        ),
        out_specs=P("exp", "ctx", None),
        check_vma=False,
    )
```

```python
import functools

import jax
import jax.numpy as jnp
from jax import lax
from jax.experimental import pallas as pl
from jax.experimental.pallas import tpu as pltpu
from jax.sharding import PartitionSpec as P

D = 2048
HEADS = 16
HEAD_DIM = 128
ROWS = 128
EXPERTS = 16
CAP = 72
SLOTS = EXPERTS * CAP
FF = 768
HALF = D // 2
Z = 8
SEG_ROWS = 16
PART = ROWS + SEG_ROWS
KEYS = 9 * ROWS
MASKED = -1e30
BF16 = jnp.bfloat16
F32 = jnp.float32

VM = pl.BlockSpec(memory_space=pltpu.VMEM)
SM = pl.BlockSpec(memory_space=pltpu.SMEM)
ANY = pl.BlockSpec(memory_space=pl.ANY)
HBM = pl.BlockSpec(memory_space=pltpu.HBM)


class Copies:
    def __init__(self, sems):
        self.sems, self.made = sems, []

    def start(self, src, dst):
        copy = pltpu.make_async_copy(src, dst, self.sems.at[len(self.made)])
        copy.start()
        self.made.append(copy)
        return copy

    def finish(self):
        for copy in self.made:
            copy.wait()


def params(mib, **kw):
    return pltpu.CompilerParams(vmem_limit_bytes=mib << 20, **kw)


def exp_pairs(f):
    pairs = []
    for e in range(16):
        y, x, c = f(e // 8, (e // 2) % 4, e % 2)
        pairs.append((e, (y % 2) * 8 + (x % 4) * 2 + c % 2))
    return pairs


CORE_SWAP = exp_pairs(lambda y, x, c: (y, x, c + 1))
Y_SWAP = exp_pairs(lambda y, x, c: (y + 1, x, c))
X_GROUPS = [[y * 8 + x * 2 + c for x in range(4)] for y in range(2) for c in range(2)]
Z_GROUPS = [list(range(8)), list(range(8, 16))]


def swap(v):
    return lax.ppermute(v, "exp", CORE_SWAP)


def y_swap(v):
    return lax.ppermute(v, "exp", Y_SWAP)


def x_exchange(v):
    return lax.all_to_all(
        v, "exp", split_axis=0, concat_axis=0, tiled=True, axis_index_groups=X_GROUPS
    )


def pair_kernel(first_ref, second_ref, out_ref, sems):
    copies = Copies(sems)
    for x in range(4):
        copies.start(first_ref, out_ref.at[x, 0])
        copies.start(second_ref, out_ref.at[x, 1])
    copies.finish()


def x_spread_pair(first, second):
    sent = pl.pallas_call(
        pair_kernel,
        out_shape=jax.ShapeDtypeStruct((4, 2) + first.shape, BF16),
        in_specs=[ANY, ANY],
        out_specs=HBM,
        scratch_shapes=[pltpu.SemaphoreType.DMA((8,))],
        compiler_params=params(60),
        cost_estimate=pl.CostEstimate(flops=0, bytes_accessed=4 << 20, transcendentals=0),
    )(first, second)
    return x_exchange(sent)


def right_kernel(w_ref, out_ref, sems):
    copies = Copies(sems)
    for x in range(4):
        copies.start(w_ref.at[:, pl.ds(HALF, HALF)], out_ref.at[x])
    copies.finish()


def x_spread_right(w):
    sent = pl.pallas_call(
        right_kernel,
        out_shape=jax.ShapeDtypeStruct((4, ROWS, HALF), BF16),
        in_specs=[ANY],
        out_specs=HBM,
        scratch_shapes=[pltpu.SemaphoreType.DMA((4,))],
        compiler_params=params(60),
        cost_estimate=pl.CostEstimate(flops=0, bytes_accessed=2 << 20, transcendentals=0),
    )(w)
    return x_exchange(sent)


def gather_weight(w, extra):
    first = jnp.concatenate([w[:, :HALF], extra], axis=0)
    first_y = y_swap(first)
    second_x = x_spread_right(w)
    first_y, second_x = lax.optimization_barrier((first_y, second_x))
    second_y = y_swap(second_x)
    first_all = x_spread_pair(first, first_y)
    second_x_other = swap(second_x)
    first_all, second_y = lax.optimization_barrier((first_all, second_y))
    return (first_all, second_x, second_y), (swap(first_all), second_x_other, swap(second_y))


def gate_rows(ids, gates):
    same = ids[None, :, :] == jnp.arange(EXPERTS, dtype=jnp.int32)[:, None, None]
    table = jnp.sum(jnp.where(same, gates[None], 0.0), axis=2)
    high = table.astype(BF16)
    low = (table - high.astype(F32)).astype(BF16)
    flat = jnp.concatenate([high.reshape(2, HALF), low.reshape(2, HALF)], axis=0)
    return jnp.pad(flat, ((0, 4), (0, 0)))


def own_gates(rows, expert):
    at = (expert % 8) * ROWS
    high = lax.dynamic_slice(rows, (0, 0, ROWS + expert // 8, at), (4, 2, 1, ROWS))
    low = lax.dynamic_slice(rows, (0, 0, ROWS + 2 + expert // 8, at), (4, 2, 1, ROWS))
    return (high.astype(F32) + low.astype(F32)).reshape(8, ROWS)


def attention_kernel(place, q_hbm, kv_hbm, qseg_ref, out_ref, q_ref, kcat, segs, bias, sems):
    z, hi, y, c = place[0], place[1], place[2], place[3]
    copies = Copies(sems)
    firsts = []
    for j in range(9):
        if j < 8:
            upper = (z < j).astype(jnp.int32)
            at = j * (2 * PART) + (1 - upper) * PART
            first = jnp.where(
                upper == 1, jnp.where(hi == 1, j * ROWS, 1 << 20), (hi * Z + j) * ROWS
            )
        else:
            at = z * (2 * PART)
            first = jnp.where(hi == 1, z * ROWS, 1 << 20)
        firsts.append(first)
        at = pl.multiple_of(at, 16)
        copies.start(kv_hbm.at[pl.ds(at, ROWS), :], kcat.at[pl.ds(j * ROWS, ROWS), :])
        copies.start(
            kv_hbm.at[pl.ds(pl.multiple_of(at + ROWS, 16), SEG_ROWS), pl.ds(0, ROWS)], segs.at[j]
        )
    copies.start(q_hbm, q_ref)
    copies.finish()
    qpos = (hi * Z + z) * ROWS + lax.broadcasted_iota(jnp.int32, (ROWS, ROWS), 0)
    lane = lax.broadcasted_iota(jnp.int32, (ROWS, ROWS), 1)
    qseg = qseg_ref[...]
    for j in range(9):
        kseg = segs[j].astype(F32)[0:1, :]
        visible = (firsts[j] + lane <= qpos) & (kseg == qseg)
        bias[:, pl.ds(j * ROWS, ROWS)] = jnp.where(visible, F32(0.0), F32(MASKED))
    scale = HEAD_DIM ** (-0.5)
    for rel in range(2):
        for yy in range(2):
            kvh = lax.rem(y + yy, 2)
            base = kvh * 8 + lax.rem(c + rel, 2)
            qs = jnp.concatenate(
                [
                    q_ref[:, pl.ds(pl.multiple_of((base + 2 * x) * HEAD_DIM, 128), HEAD_DIM)]
                    for x in range(4)
                ],
                axis=0,
            )
            k = kcat[:, pl.ds(pl.multiple_of(kvh * HEAD_DIM, 128), HEAD_DIM)]
            v = kcat[:, pl.ds(pl.multiple_of(256 + kvh * HEAD_DIM, 128), HEAD_DIM)]
            s = lax.dot_general(qs, k, (((1,), (1,)), ((), ())), preferred_element_type=F32)
            s = s.reshape(4, ROWS, KEYS) * scale + bias[...][None]
            top = jnp.max(s, axis=-1, keepdims=True)
            w = jnp.exp(s - top)
            total = jnp.sum(w, axis=-1, keepdims=True).reshape(4 * ROWS, 1)
            a = jnp.dot(
                w.astype(BF16).reshape(4 * ROWS, KEYS), v, preferred_element_type=F32
            )
            a = (a / total).astype(BF16)
            for x in range(4):
                out_ref[:, pl.ds(rel * HALF + (2 * x + yy) * HEAD_DIM, HEAD_DIM)] = a[
                    x * ROWS : (x + 1) * ROWS
                ]


def attention(place, q, kv, qseg):
    return pl.pallas_call(
        attention_kernel,
        out_shape=jax.ShapeDtypeStruct((ROWS, D), BF16),
        in_specs=[SM, ANY, ANY, VM],
        out_specs=VM,
        scratch_shapes=[
            pltpu.VMEM((ROWS, D), BF16),
            pltpu.VMEM((KEYS, 512), BF16),
            pltpu.VMEM((9, SEG_ROWS, ROWS), BF16),
            pltpu.VMEM((ROWS, KEYS), F32),
            pltpu.SemaphoreType.DMA((19,)),
        ],
        compiler_params=params(60),
        cost_estimate=pl.CostEstimate(
            flops=4 * HEADS * ROWS * KEYS * HEAD_DIM,
            bytes_accessed=4 << 20,
            transcendentals=HEADS * ROWS * KEYS,
        ),
    )(place, q, kv, qseg)


def project_kernel(
    att_ref, fo, sox, soy, fx, sxx, sxy, res_ref, gain_ref,
    hid_hbm, first_hbm, second_hbm,
    hid_ref, first_ref, second_ref, wl, wr, sems, w_sems,
):
    copies, fetched = Copies(sems), Copies(w_sems)
    for half, a_hbm, x_hbm, y_hbm in ((0, fo, sox, soy), (1, fx, sxx, sxy)):
        for x in range(4):
            for yy in range(2):
                at = pl.ds(half * HALF + (2 * x + yy) * ROWS, ROWS)
                fetched.start(a_hbm.at[x, yy, pl.ds(0, ROWS), :], wl.at[at, :])
                fetched.start((y_hbm if yy else x_hbm).at[x], wr.at[at, :])
    left = jnp.zeros((ROWS, HALF), F32)
    right = jnp.zeros((ROWS, HALF), F32)
    for part in range(4):
        for copy in fetched.made[8 * part : 8 * part + 8]:
            copy.wait()
        at = pl.ds(part * 512, 512)
        left = left + jnp.dot(att_ref[:, at], wl[at, :], preferred_element_type=F32)
        right = right + jnp.dot(att_ref[:, at], wr[at, :], preferred_element_type=F32)
    left = left + res_ref[:, :HALF].astype(F32)
    right = right + res_ref[:, HALF:].astype(F32)
    hid_ref[:, :HALF] = left
    hid_ref[:, HALF:] = right
    copies.start(hid_ref, hid_hbm)
    square = jnp.sum(left * left, axis=-1, keepdims=True) + jnp.sum(
        right * right, axis=-1, keepdims=True
    )
    scale = lax.rsqrt(square * (1.0 / D) + 1e-06)
    gain = gain_ref[...]
    first_ref[...] = (left * scale * gain[:, :HALF]).astype(BF16)
    copies.start(first_ref, first_hbm)
    second_ref[...] = (right * scale * gain[:, HALF:]).astype(BF16)
    for x in range(4):
        copies.start(second_ref, second_hbm.at[x])
    copies.finish()


def project(att, own, other, residual, gain):
    return pl.pallas_call(
        project_kernel,
        out_shape=(
            jax.ShapeDtypeStruct((ROWS, D), F32),
            jax.ShapeDtypeStruct((ROWS, HALF), BF16),
            jax.ShapeDtypeStruct((4, ROWS, HALF), BF16),
        ),
        in_specs=[VM] + [ANY] * 6 + [VM] * 2,
        out_specs=(HBM, HBM, HBM),
        scratch_shapes=[
            pltpu.VMEM((ROWS, D), F32),
            pltpu.VMEM((ROWS, HALF), BF16),
            pltpu.VMEM((ROWS, HALF), BF16),
            pltpu.VMEM((D, HALF), BF16),
            pltpu.VMEM((D, HALF), BF16),
            pltpu.SemaphoreType.DMA((6,)),
            pltpu.SemaphoreType.DMA((32,)),
        ],
        compiler_params=params(60),
        cost_estimate=pl.CostEstimate(
            flops=2 * ROWS * D * D, bytes_accessed=11 << 20, transcendentals=ROWS
        ),
    )(att, *own, *other, residual, gain)


def pick_rows(gates):
    named = (gates > 0.0).astype(F32)
    before = (
        lax.broadcasted_iota(jnp.int32, (ROWS, ROWS), 0)
        < lax.broadcasted_iota(jnp.int32, (ROWS, ROWS), 1)
    ).astype(BF16)
    rank = jnp.dot(named.astype(BF16), before, preferred_element_type=F32)
    rank = jnp.where(named > 0.5, rank, F32(-1.0))
    row = lax.broadcasted_iota(jnp.int32, (2 * CAP, 2 * ROWS), 0)
    lane = lax.broadcasted_iota(jnp.int32, (2 * CAP, 2 * ROWS), 1)
    second = row >= CAP
    slot = jnp.where(second, row - CAP, row)
    slot = jnp.where(second == (lane >= ROWS), slot, -2).astype(F32)
    picks, scales = [], []
    for x in range(4):
        both = jnp.concatenate([rank[2 * x : 2 * x + 1], rank[2 * x + 1 : 2 * x + 2]], axis=1)
        here = (both == slot).astype(F32)
        gate = jnp.concatenate([gates[2 * x : 2 * x + 1], gates[2 * x + 1 : 2 * x + 2]], axis=1)
        scales.append(jnp.sum(here * gate, axis=1, keepdims=True))
        picks.append(here.astype(BF16))
    return picks, scales


def fetch_tokens(copies, a_hbm, bx_hbm, by_hbm, tokens):
    fetched = []
    for x in range(4):
        fetched.append(
            [
                copies.start(a_hbm.at[x], tokens.at[0, x]),
                copies.start(bx_hbm.at[x], tokens.at[1, x, 0]),
                copies.start(by_hbm.at[x], tokens.at[1, x, 1]),
            ]
        )
    return fetched


def activate(picks, fetched, tokens, fetched_g, g_ref, fetched_u, u_ref, rows):
    for x in range(4):
        for copy in fetched[x]:
            copy.wait()
        left = tokens[0, x].reshape(2 * ROWS, HALF)
        right = tokens[1, x].reshape(2 * ROWS, HALF)
        left = jnp.dot(picks[x], left, preferred_element_type=F32)
        right = jnp.dot(picks[x], right, preferred_element_type=F32)
        rows[pl.ds(x * 2 * CAP, 2 * CAP), :HALF] = left.astype(BF16)
        rows[pl.ds(x * 2 * CAP, 2 * CAP), HALF:] = right.astype(BF16)
    fetched_g.wait()
    gate = jnp.dot(rows[...], g_ref[...], preferred_element_type=F32)
    fetched_u.wait()
    up = jnp.dot(rows[...], u_ref[...], preferred_element_type=F32)
    return (gate / (1.0 + jnp.exp(-gate)) * up).astype(BF16)


def gated_blocks(x, picks, scales, activ, d_ref):
    o = jnp.dot(activ[x * 2 * CAP : (x + 1) * 2 * CAP], d_ref[...], preferred_element_type=F32)
    o = (o * scales[x]).astype(BF16)
    return lax.dot_general(picks[x], o, (((0,), (0,)), ((), ())), preferred_element_type=F32)


def other_kernel(
    a_hbm, bx_hbm, by_hbm, gate_ref, g_hbm, u_hbm, d_hbm, out_hbm,
    tokens, rows, g_ref, u_ref, d_ref, out_ref, sems, out_sems,
):
    copies, results = Copies(sems), Copies(out_sems)
    fetched = fetch_tokens(copies, a_hbm, bx_hbm, by_hbm, tokens)
    fetched_g = copies.start(g_hbm, g_ref)
    fetched_u = copies.start(u_hbm, u_ref)
    fetched_d = copies.start(d_hbm, d_ref)
    picks, scales = pick_rows(gate_ref[...])
    activ = activate(picks, fetched, tokens, fetched_g, g_ref, fetched_u, u_ref, rows)
    fetched_d.wait()
    for x in range(4):
        dense = gated_blocks(x, picks, scales, activ, d_ref).astype(BF16)
        for yy in range(2):
            out_ref[0, x, yy] = dense[yy * ROWS : (yy + 1) * ROWS, :HALF]
            out_ref[1, x, yy] = dense[yy * ROWS : (yy + 1) * ROWS, HALF:]
        for side in range(2):
            results.start(out_ref.at[side, x], out_hbm.at[side, x])
    results.finish()


def own_up_kernel(
    a_hbm, bx_hbm, by_hbm, gate_ref, g_hbm, u_hbm, out_ref, tokens, rows, g_ref, u_ref, sems
):
    copies = Copies(sems)
    fetched = fetch_tokens(copies, a_hbm, bx_hbm, by_hbm, tokens)
    fetched_g = copies.start(g_hbm, g_ref)
    fetched_u = copies.start(u_hbm, u_ref)
    picks, _ = pick_rows(gate_ref[...])
    out_ref[...] = activate(picks, fetched, tokens, fetched_g, g_ref, fetched_u, u_ref, rows)


def own_down_kernel(
    activ_ref, gate_ref, d_ref, add_hbm, keep_ref, send_hbm, both_hbm,
    add_ref, send_ref, both_ref, sems, out_sems,
):
    copies, results = Copies(sems), Copies(out_sems)
    fetched = [
        [copies.start(add_hbm.at[side, x], add_ref.at[side, x]) for side in range(2)]
        for x in range(4)
    ]
    picks, scales = pick_rows(gate_ref[...])
    activ = activ_ref[...]
    for x in range(4):
        dense = gated_blocks(x, picks, scales, activ, d_ref)
        for copy in fetched[x]:
            copy.wait()
        for yy in range(2):
            d = dense[yy * ROWS : (yy + 1) * ROWS]
            part = (d[:, :HALF] + add_ref[0, x, yy].astype(F32)).astype(BF16)
            (send_ref if yy else keep_ref)[x] = part
            both_ref[x, yy] = (d[:, HALF:] + add_ref[1, x, yy].astype(F32)).astype(BF16)
        results.start(send_ref.at[x], send_hbm.at[x])
        results.start(both_ref.at[x], both_hbm.at[x])
    results.finish()


PICKED = SLOTS // 2
TOKENS = pltpu.VMEM((2, 4, 2, ROWS, HALF), BF16)
PICKED_ROWS = pltpu.VMEM((PICKED, D), BF16)
UP = pltpu.VMEM((D, FF), BF16)
DOWN = pltpu.VMEM((FF, D), BF16)
DMA = pltpu.SemaphoreType.DMA


def shape(*dims, dtype=BF16):
    return jax.ShapeDtypeStruct(dims, dtype)


def kernel_call(body, out_shape, in_specs, out_specs, mib, flops, moved, scratch=()):
    return pl.pallas_call(
        body,
        out_shape=out_shape,
        in_specs=in_specs,
        out_specs=out_specs,
        scratch_shapes=scratch,
        compiler_params=params(mib),
        cost_estimate=pl.CostEstimate(flops=flops, bytes_accessed=moved, transcendentals=0),
    )


def experts_other(tokens, gates, w_gate, w_up, w_down):
    return kernel_call(
        other_kernel,
        shape(2, 4, 2, ROWS, HALF),
        [ANY, ANY, ANY, VM, ANY, ANY, ANY],
        HBM,
        60,
        6 * PICKED * D * FF,
        16 << 20,
        [TOKENS, PICKED_ROWS, UP, UP, DOWN, TOKENS, DMA((15,)), DMA((8,))],
    )(*tokens, gates, w_gate, w_up, w_down)


def experts_own_up(tokens, gates, w_gate, w_up):
    return kernel_call(
        own_up_kernel,
        shape(PICKED, FF),
        [ANY, ANY, ANY, VM, ANY, ANY],
        VM,
        60,
        4 * PICKED * D * FF,
        10 << 20,
        [TOKENS, PICKED_ROWS, UP, UP, DMA((14,))],
    )(*tokens, gates, w_gate, w_up)


def experts_own_down(activ, gates, w_down, add):
    half, whole = (4, ROWS, HALF), (4, 2, ROWS, HALF)
    return kernel_call(
        own_down_kernel,
        (shape(*half), shape(*half), shape(*whole)),
        [VM, VM, VM, ANY],
        (VM, HBM, HBM),
        60,
        2 * PICKED * D * FF,
        12 << 20,
        [TOKENS, pltpu.VMEM(half, BF16), pltpu.VMEM(whole, BF16), DMA((8,)), DMA((8,))],
    )(activ, gates, w_down, add)


def final_kernel(hid_ref, x_ref, b_ref, y_ref, out_ref):
    left = hid_ref[:, :HALF]
    for x in range(4):
        left = left + x_ref[x].astype(F32)
    out_ref[:, :HALF] = left.astype(BF16)
    right = hid_ref[:, HALF:] + (b_ref[...] + y_ref[...].astype(F32))
    out_ref[:, HALF:] = right.astype(BF16)


def spread_tokens(first, second):
    first_y = y_swap(first)
    second_x = x_exchange(second)
    first_y, second_x = lax.optimization_barrier((first_y, second_x))
    second_y = y_swap(second_x)
    first_all = x_spread_pair(first, first_y)
    own = (first_all, second_x, second_y)
    return own, tuple(swap(v) for v in own)


def reduce_back(keep, send, both, hidden):
    got_y = y_swap(send)
    got_x = x_exchange(both)
    part_a = (keep.astype(F32) + got_y.astype(F32)).astype(BF16)
    part_b = jnp.sum(got_x.astype(F32), axis=0)
    last_y = y_swap(part_b[1].astype(BF16))
    last_x = x_exchange(part_a)
    return kernel_call(final_kernel, shape(ROWS, D), [VM] * 4, VM, 12, ROWS * D, 4 << 20)(
        hidden, last_x, part_b[0], last_y
    )


def per_device(
    queries,
    keys,
    values,
    segments,
    residual,
    out_weight,
    norm_gain,
    expert_ids,
    gate_weights,
    w_gate,
    w_up,
    w_down,
):
    ctx, exp = lax.axis_index("ctx"), lax.axis_index("exp")
    place = jnp.stack([ctx % Z, ctx // Z, exp // 8, exp % 2]).astype(jnp.int32)
    seg_rows = jnp.broadcast_to(
        jnp.pad(segments.astype(BF16), ((0, 0), (0, 512 - ROWS))), (SEG_ROWS, 512)
    )
    own = jnp.concatenate(
        [jnp.concatenate([keys[0], values[0]], axis=1), seg_rows], axis=0
    )
    upper = lax.ppermute(own, "ctx", [(s, s + Z) for s in range(Z)])
    kv = lax.all_gather(
        jnp.concatenate([upper, own], axis=0),
        "ctx",
        axis=0,
        tiled=True,
        axis_index_groups=Z_GROUPS,
    )
    weight, weight_other = gather_weight(
        out_weight, gate_rows(expert_ids[0], gate_weights[0])
    )
    att = attention(place, queries[0], kv, segments[0].astype(F32)[:, None])
    hidden, first, second = project(att, weight, weight_other, residual[0], norm_gain[None, :])
    own, other = spread_tokens(first, second)
    gates, gates_other = own_gates(weight[0], exp), own_gates(weight_other[0], exp)
    partial = swap(experts_other(other, gates_other, w_gate[0], w_up[0], w_down[0]))
    activ = experts_own_up(own, gates, w_gate[0], w_up[0])
    keep, send, both = experts_own_down(activ, gates, w_down[0], partial)
    return reduce_back(keep, send, both, hidden)[None]


def solution(mesh):
    return jax.shard_map(
        per_device,
        mesh=mesh,
        in_specs=(
            P("exp", "ctx", None),
            P("exp", "ctx", None),
            P("exp", "ctx", None),
            P("exp", "ctx"),
            P("exp", "ctx", None),
            P("exp", None),
            P(),
            P("exp", "ctx", None),
            P("exp", "ctx", None),
            P("exp", None, None),
            P("exp", None, None),
            P("exp", None, None),
        ),
        out_specs=P("exp", "ctx", None),
        check_vma=False,
    )
```

```python
import functools

import jax
import jax.numpy as jnp
from jax import lax
from jax.experimental import pallas as pl
from jax.experimental.pallas import tpu as pltpu
from jax.sharding import PartitionSpec as P

D = 2048
HEADS = 16
HEAD_DIM = 128
ROWS = 128
EXPERTS = 16
CAP = 72
SLOTS = EXPERTS * CAP
FF = 768
HALF = D // 2
Z = 8
SEG_ROWS = 16
PART = ROWS + SEG_ROWS
KEYS = 9 * ROWS
MASKED = -1e30
BF16 = jnp.bfloat16
F32 = jnp.float32

VM = pl.BlockSpec(memory_space=pltpu.VMEM)
SM = pl.BlockSpec(memory_space=pltpu.SMEM)


def params(mib, **kw):
    return pltpu.CompilerParams(vmem_limit_bytes=mib << 20, **kw)


def exp_pairs(f):
    pairs = []
    for e in range(16):
        y, x, c = f(e // 8, (e // 2) % 4, e % 2)
        pairs.append((e, (y % 2) * 8 + (x % 4) * 2 + c % 2))
    return pairs


CORE_SWAP = exp_pairs(lambda y, x, c: (y, x, c + 1))
Y_SWAP = exp_pairs(lambda y, x, c: (y + 1, x, c))
X_GROUPS = [[y * 8 + x * 2 + c for x in range(4)] for y in range(2) for c in range(2)]
Z_GROUPS = [list(range(8)), list(range(8, 16))]


def swap(v):
    return lax.ppermute(v, "exp", CORE_SWAP)


def y_swap(v):
    return lax.ppermute(v, "exp", Y_SWAP)


def x_exchange(v):
    return lax.all_to_all(
        v, "exp", split_axis=0, concat_axis=0, tiled=True, axis_index_groups=X_GROUPS
    )


def x_spread(v):
    return x_exchange(jnp.broadcast_to(v[None], (4,) + v.shape))


def gather_weight(w, extra):
    first = jnp.concatenate([w[:, :HALF], extra], axis=0)
    first_y = y_swap(first)
    second_x = x_spread(w[:, HALF:])
    first_y, second_x = lax.optimization_barrier((first_y, second_x))
    second_y = y_swap(second_x)
    first_all = x_spread(jnp.stack([first, first_y]))
    second_x_other = swap(second_x)
    first_all, second_y = lax.optimization_barrier((first_all, second_y))
    return (first_all, second_x, second_y), (swap(first_all), second_x_other, swap(second_y))


def gate_rows(ids, gates):
    same = ids[None, :, :] == jnp.arange(EXPERTS, dtype=jnp.int32)[:, None, None]
    table = jnp.sum(jnp.where(same, gates[None], 0.0), axis=2)
    high = table.astype(BF16)
    low = (table - high.astype(F32)).astype(BF16)
    flat = jnp.concatenate([high.reshape(2, HALF), low.reshape(2, HALF)], axis=0)
    return jnp.pad(flat, ((0, 4), (0, 0)))


def own_gates(rows, expert):
    at = (expert % 8) * ROWS
    high = lax.dynamic_slice(rows, (0, 0, ROWS + expert // 8, at), (4, 2, 1, ROWS))
    low = lax.dynamic_slice(rows, (0, 0, ROWS + 2 + expert // 8, at), (4, 2, 1, ROWS))
    return (high.astype(F32) + low.astype(F32)).reshape(8, ROWS)


def attention_kernel(place, q_ref, kv_ref, qseg_ref, out_ref, kcat, bias):
    z, hi, y, c = place[0], place[1], place[2], place[3]
    qpos = (hi * Z + z) * ROWS + lax.broadcasted_iota(jnp.int32, (ROWS, ROWS), 0)
    lane = lax.broadcasted_iota(jnp.int32, (ROWS, ROWS), 1)
    qseg = qseg_ref[...]
    for j in range(9):
        if j < 8:
            upper = (z < j).astype(jnp.int32)
            at = j * (2 * PART) + (1 - upper) * PART
            first = jnp.where(
                upper == 1, jnp.where(hi == 1, j * ROWS, 1 << 20), (hi * Z + j) * ROWS
            )
        else:
            at = z * (2 * PART)
            first = jnp.where(hi == 1, z * ROWS, 1 << 20)
        at = pl.multiple_of(at, 16)
        kcat[pl.ds(j * ROWS, ROWS), :] = kv_ref[pl.ds(at, ROWS), :]
        kseg = kv_ref[pl.ds(pl.multiple_of(at + ROWS, 16), SEG_ROWS), 0:ROWS].astype(F32)[0:1, :]
        visible = (first + lane <= qpos) & (kseg == qseg)
        bias[:, pl.ds(j * ROWS, ROWS)] = jnp.where(visible, F32(0.0), F32(MASKED))
    scale = HEAD_DIM ** (-0.5)
    for rel in range(2):
        for yy in range(2):
            kvh = lax.rem(y + yy, 2)
            base = kvh * 8 + lax.rem(c + rel, 2)
            qs = jnp.concatenate(
                [
                    q_ref[:, pl.ds(pl.multiple_of((base + 2 * x) * HEAD_DIM, 128), HEAD_DIM)]
                    for x in range(4)
                ],
                axis=0,
            )
            k = kcat[:, pl.ds(pl.multiple_of(kvh * HEAD_DIM, 128), HEAD_DIM)]
            v = kcat[:, pl.ds(pl.multiple_of(256 + kvh * HEAD_DIM, 128), HEAD_DIM)]
            s = lax.dot_general(qs, k, (((1,), (1,)), ((), ())), preferred_element_type=F32)
            s = s.reshape(4, ROWS, KEYS) * scale + bias[...][None]
            top = jnp.max(s, axis=-1, keepdims=True)
            w = jnp.exp(s - top)
            total = jnp.sum(w, axis=-1, keepdims=True).reshape(4 * ROWS, 1)
            a = jnp.dot(
                w.astype(BF16).reshape(4 * ROWS, KEYS), v, preferred_element_type=F32
            )
            a = (a / total).astype(BF16)
            for x in range(4):
                out_ref[:, pl.ds(rel * HALF + (2 * x + yy) * HEAD_DIM, HEAD_DIM)] = a[
                    x * ROWS : (x + 1) * ROWS
                ]


def attention(place, q, kv, qseg):
    return pl.pallas_call(
        attention_kernel,
        out_shape=jax.ShapeDtypeStruct((ROWS, D), BF16),
        in_specs=[SM, VM, VM, VM],
        out_specs=VM,
        scratch_shapes=[pltpu.VMEM((KEYS, 512), BF16), pltpu.VMEM((ROWS, KEYS), F32)],
        compiler_params=params(24),
        cost_estimate=pl.CostEstimate(
            flops=4 * HEADS * ROWS * KEYS * HEAD_DIM,
            bytes_accessed=4 << 20,
            transcendentals=HEADS * ROWS * KEYS,
        ),
    )(place, q, kv, qseg)


def right_rows(x_ref, y_ref):
    parts = []
    for x in range(4):
        parts += [x_ref[x], y_ref[x]]
    return jnp.concatenate(parts, axis=0)


def project_kernel(
    att_ref, fo, sox, soy, fx, sxx, sxy, res_ref, gain_ref, hid_ref, first_ref, second_ref
):
    own, other = att_ref[:, :HALF], att_ref[:, HALF:]
    fo_rows = fo[:, :, 0:ROWS, :].reshape(HALF, HALF)
    fx_rows = fx[:, :, 0:ROWS, :].reshape(HALF, HALF)
    left = jnp.dot(own, fo_rows, preferred_element_type=F32) + jnp.dot(
        other, fx_rows, preferred_element_type=F32
    )
    right = jnp.dot(own, right_rows(sox, soy), preferred_element_type=F32) + jnp.dot(
        other, right_rows(sxx, sxy), preferred_element_type=F32
    )
    left = left + res_ref[:, :HALF].astype(F32)
    right = right + res_ref[:, HALF:].astype(F32)
    hid_ref[:, :HALF] = left
    hid_ref[:, HALF:] = right
    square = jnp.sum(left * left, axis=-1, keepdims=True) + jnp.sum(
        right * right, axis=-1, keepdims=True
    )
    scale = lax.rsqrt(square * (1.0 / D) + 1e-06)
    gain = gain_ref[...]
    first_ref[...] = (left * scale * gain[:, :HALF]).astype(BF16)
    second = (right * scale * gain[:, HALF:]).astype(BF16)
    for x in range(4):
        second_ref[x] = second


def project(att, own, other, residual, gain):
    return pl.pallas_call(
        project_kernel,
        out_shape=(
            jax.ShapeDtypeStruct((ROWS, D), F32),
            jax.ShapeDtypeStruct((ROWS, HALF), BF16),
            jax.ShapeDtypeStruct((4, ROWS, HALF), BF16),
        ),
        in_specs=[VM] * 9,
        out_specs=(VM, VM, VM),
        compiler_params=params(50),
        cost_estimate=pl.CostEstimate(
            flops=2 * ROWS * D * D, bytes_accessed=11 << 20, transcendentals=ROWS
        ),
    )(att, *own, *other, residual, gain)


def pick_rows(gates):
    named = (gates > 0.0).astype(F32)
    before = (
        lax.broadcasted_iota(jnp.int32, (ROWS, ROWS), 0)
        < lax.broadcasted_iota(jnp.int32, (ROWS, ROWS), 1)
    ).astype(BF16)
    rank = jnp.dot(named.astype(BF16), before, preferred_element_type=F32)
    rank = jnp.where(named > 0.5, rank, F32(-1.0))
    row = lax.broadcasted_iota(jnp.int32, (2 * CAP, 2 * ROWS), 0)
    lane = lax.broadcasted_iota(jnp.int32, (2 * CAP, 2 * ROWS), 1)
    second = row >= CAP
    slot = jnp.where(second, row - CAP, row)
    slot = jnp.where(second == (lane >= ROWS), slot, -2).astype(F32)
    picks, scales = [], []
    for x in range(4):
        both = jnp.concatenate([rank[2 * x : 2 * x + 1], rank[2 * x + 1 : 2 * x + 2]], axis=1)
        here = (both == slot).astype(F32)
        gate = jnp.concatenate([gates[2 * x : 2 * x + 1], gates[2 * x + 1 : 2 * x + 2]], axis=1)
        scales.append(jnp.sum(here * gate, axis=1, keepdims=True))
        picks.append(here.astype(BF16))
    return picks, scales


def activate(picks, a_ref, bx_ref, by_ref, g_ref, u_ref, rows):
    for x in range(4):
        left = jnp.dot(picks[x], a_ref[x].reshape(2 * ROWS, HALF), preferred_element_type=F32)
        tokens = jnp.concatenate([bx_ref[x], by_ref[x]], axis=0)
        right = jnp.dot(picks[x], tokens, preferred_element_type=F32)
        rows[pl.ds(x * 2 * CAP, 2 * CAP), :HALF] = left.astype(BF16)
        rows[pl.ds(x * 2 * CAP, 2 * CAP), HALF:] = right.astype(BF16)
    gate = jnp.dot(rows[...], g_ref[...], preferred_element_type=F32)
    up = jnp.dot(rows[...], u_ref[...], preferred_element_type=F32)
    return (gate / (1.0 + jnp.exp(-gate)) * up).astype(BF16)


def gated_blocks(x, picks, scales, activ, d_ref):
    o = jnp.dot(activ[x * 2 * CAP : (x + 1) * 2 * CAP], d_ref[...], preferred_element_type=F32)
    o = (o * scales[x]).astype(BF16)
    return lax.dot_general(picks[x], o, (((0,), (0,)), ((), ())), preferred_element_type=F32)


def other_kernel(a_ref, bx_ref, by_ref, gate_ref, g_ref, u_ref, d_ref, out_ref, rows):
    picks, scales = pick_rows(gate_ref[...])
    activ = activate(picks, a_ref, bx_ref, by_ref, g_ref, u_ref, rows)
    for x in range(4):
        dense = gated_blocks(x, picks, scales, activ, d_ref).astype(BF16)
        for yy in range(2):
            out_ref[0, x, yy] = dense[yy * ROWS : (yy + 1) * ROWS, :HALF]
            out_ref[1, x, yy] = dense[yy * ROWS : (yy + 1) * ROWS, HALF:]


def own_up_kernel(a_ref, bx_ref, by_ref, gate_ref, g_ref, u_ref, out_ref, rows):
    picks, _ = pick_rows(gate_ref[...])
    out_ref[...] = activate(picks, a_ref, bx_ref, by_ref, g_ref, u_ref, rows)


def own_down_kernel(activ_ref, gate_ref, d_ref, add_ref, keep_ref, send_ref, both_ref):
    picks, scales = pick_rows(gate_ref[...])
    activ = activ_ref[...]
    for x in range(4):
        dense = gated_blocks(x, picks, scales, activ, d_ref)
        for yy in range(2):
            d = dense[yy * ROWS : (yy + 1) * ROWS]
            part = (d[:, :HALF] + add_ref[0, x, yy].astype(F32)).astype(BF16)
            (send_ref if yy else keep_ref)[x] = part
            both_ref[x, yy] = (d[:, HALF:] + add_ref[1, x, yy].astype(F32)).astype(BF16)


PICKED = SLOTS // 2
ROW_SCRATCH = pltpu.VMEM((PICKED, D), BF16)


def kernel_call(body, out_shape, mib, flops, moved, scratch=()):
    many = isinstance(out_shape, tuple)

    def call(*operands):
        return pl.pallas_call(
            body,
            out_shape=out_shape,
            in_specs=[VM] * len(operands),
            out_specs=(VM,) * len(out_shape) if many else VM,
            scratch_shapes=scratch,
            compiler_params=params(mib),
            cost_estimate=pl.CostEstimate(flops=flops, bytes_accessed=moved, transcendentals=0),
        )(*operands)

    return call


def shape(*dims, dtype=BF16):
    return jax.ShapeDtypeStruct(dims, dtype)


def experts_other(tokens, gates, w_gate, w_up, w_down):
    return kernel_call(
        other_kernel,
        shape(2, 4, 2, ROWS, HALF),
        30,
        6 * PICKED * D * FF,
        16 << 20,
        [ROW_SCRATCH],
    )(*tokens, gates, w_gate, w_up, w_down)


def experts_own_up(tokens, gates, w_gate, w_up):
    return kernel_call(
        own_up_kernel, shape(PICKED, FF), 24, 4 * PICKED * D * FF, 10 << 20, [ROW_SCRATCH]
    )(*tokens, gates, w_gate, w_up)


def experts_own_down(activ, gates, w_down, add):
    return kernel_call(
        own_down_kernel,
        (shape(4, ROWS, HALF), shape(4, ROWS, HALF), shape(4, 2, ROWS, HALF)),
        36,
        2 * PICKED * D * FF,
        12 << 20,
    )(activ, gates, w_down, add)


def final_kernel(hid_ref, x_ref, b_ref, y_ref, out_ref):
    left = hid_ref[:, :HALF]
    for x in range(4):
        left = left + x_ref[x].astype(F32)
    out_ref[:, :HALF] = left.astype(BF16)
    right = hid_ref[:, HALF:] + (b_ref[...] + y_ref[...].astype(F32))
    out_ref[:, HALF:] = right.astype(BF16)


def touch_kernel(g_ref, u_ref, d_ref, after_ref, out_ref):
    out_ref[...] = after_ref[...]


def touch(matrices, after):
    return kernel_call(touch_kernel, shape(*after.shape, dtype=F32), 4, 0, 20 << 20)(
        *matrices, after
    )


def spread_tokens(first, second):
    first_y = y_swap(first)
    second_x = x_exchange(second)
    first_y, second_x = lax.optimization_barrier((first_y, second_x))
    second_y = y_swap(second_x)
    pair = jnp.stack([first, first_y])
    first_all = x_spread(pair)
    own = (first_all, second_x, second_y)
    return own, tuple(swap(v) for v in own), pair


def reduce_back(keep, send, both, hidden):
    got_y = y_swap(send)
    got_x = x_exchange(both)
    part_a = (keep.astype(F32) + got_y.astype(F32)).astype(BF16)
    part_b = jnp.sum(got_x.astype(F32), axis=0)
    last_y = y_swap(part_b[1].astype(BF16))
    last_x = x_exchange(part_a)
    return kernel_call(final_kernel, shape(ROWS, D), 12, ROWS * D, 4 << 20)(
        hidden, last_x, part_b[0], last_y
    )


def per_device(
    queries,
    keys,
    values,
    segments,
    residual,
    out_weight,
    norm_gain,
    expert_ids,
    gate_weights,
    w_gate,
    w_up,
    w_down,
):
    ctx, exp = lax.axis_index("ctx"), lax.axis_index("exp")
    place = jnp.stack([ctx % Z, ctx // Z, exp // 8, exp % 2]).astype(jnp.int32)
    seg_rows = jnp.broadcast_to(
        jnp.pad(segments.astype(BF16), ((0, 0), (0, 512 - ROWS))), (SEG_ROWS, 512)
    )
    own = jnp.concatenate(
        [jnp.concatenate([keys[0], values[0]], axis=1), seg_rows], axis=0
    )
    upper = lax.ppermute(own, "ctx", [(s, s + Z) for s in range(Z)])
    kv = lax.all_gather(
        jnp.concatenate([upper, own], axis=0),
        "ctx",
        axis=0,
        tiled=True,
        axis_index_groups=Z_GROUPS,
    )
    weight, weight_other = gather_weight(
        out_weight, gate_rows(expert_ids[0], gate_weights[0])
    )
    att = attention(place, queries[0], kv, segments[0].astype(F32)[:, None])
    hidden, first, second = project(att, weight, weight_other, residual[0], norm_gain[None, :])
    own, other, pair = spread_tokens(first, second)
    gates, gates_other = own_gates(weight[0], exp), own_gates(weight_other[0], exp)
    gates_other, _ = lax.optimization_barrier((gates_other, pair))
    gates_other = touch((w_gate[0], w_up[0], w_down[0]), gates_other)
    partial = swap(experts_other(other, gates_other, w_gate[0], w_up[0], w_down[0]))
    activ = experts_own_up(own, gates, w_gate[0], w_up[0])
    keep, send, both = experts_own_down(activ, gates, w_down[0], partial)
    return reduce_back(keep, send, both, hidden)[None]


def solution(mesh):
    return jax.shard_map(
        per_device,
        mesh=mesh,
        in_specs=(
            P("exp", "ctx", None),
            P("exp", "ctx", None),
            P("exp", "ctx", None),
            P("exp", "ctx"),
            P("exp", "ctx", None),
            P("exp", None),
            P(),
            P("exp", "ctx", None),
            P("exp", "ctx", None),
            P("exp", None, None),
            P("exp", None, None),
            P("exp", None, None),
        ),
        out_specs=P("exp", "ctx", None),
        check_vma=False,
    )
```

```python
import functools

import jax
import jax.numpy as jnp
from jax import lax
from jax.experimental import pallas as pl
from jax.experimental.pallas import tpu as pltpu
from jax.sharding import PartitionSpec as P

D = 2048
HEADS = 16
HEAD_DIM = 128
ROWS = 128
EXPERTS = 16
CAP = 72
SLOTS = EXPERTS * CAP
FF = 768
HALF = D // 2
Z = 8
SEG_ROWS = 16
PART = ROWS + SEG_ROWS
KEYS = 9 * ROWS
MASKED = -1e30
BF16 = jnp.bfloat16
F32 = jnp.float32

VM = pl.BlockSpec(memory_space=pltpu.VMEM)
SM = pl.BlockSpec(memory_space=pltpu.SMEM)


def params(mib, **kw):
    return pltpu.CompilerParams(vmem_limit_bytes=mib << 20, **kw)


def exp_pairs(f):
    pairs = []
    for e in range(16):
        y, x, c = f(e // 8, (e // 2) % 4, e % 2)
        pairs.append((e, (y % 2) * 8 + (x % 4) * 2 + c % 2))
    return pairs


CORE_SWAP = exp_pairs(lambda y, x, c: (y, x, c + 1))
Y_SWAP = exp_pairs(lambda y, x, c: (y + 1, x, c))
X_GROUPS = [[y * 8 + x * 2 + c for x in range(4)] for y in range(2) for c in range(2)]
Z_GROUPS = [list(range(8)), list(range(8, 16))]


def swap(v):
    return lax.ppermute(v, "exp", CORE_SWAP)


def y_swap(v):
    return lax.ppermute(v, "exp", Y_SWAP)


def x_exchange(v):
    return lax.all_to_all(
        v, "exp", split_axis=0, concat_axis=0, tiled=True, axis_index_groups=X_GROUPS
    )


def x_spread(v):
    return x_exchange(jnp.broadcast_to(v[None], (4,) + v.shape))


def gather_weight(w, extra):
    first = jnp.concatenate([w[:, :HALF], extra], axis=0)
    first_y = y_swap(first)
    second_x = x_spread(w[:, HALF:])
    first_y, second_x = lax.optimization_barrier((first_y, second_x))
    second_y = y_swap(second_x)
    first_all = x_spread(jnp.stack([first, first_y]))
    second_x_other = swap(second_x)
    first_all, second_y = lax.optimization_barrier((first_all, second_y))
    return (first_all, second_x, second_y), (swap(first_all), second_x_other, swap(second_y))


def gate_rows(ids, gates):
    same = ids[None, :, :] == jnp.arange(EXPERTS, dtype=jnp.int32)[:, None, None]
    table = jnp.sum(jnp.where(same, gates[None], 0.0), axis=2)
    high = table.astype(BF16)
    low = (table - high.astype(F32)).astype(BF16)
    flat = jnp.concatenate([high.reshape(2, HALF), low.reshape(2, HALF)], axis=0)
    return jnp.pad(flat, ((0, 4), (0, 0)))


def own_gates(rows, expert):
    at = (expert % 8) * ROWS
    high = lax.dynamic_slice(rows, (0, 0, ROWS + expert // 8, at), (4, 2, 1, ROWS))
    low = lax.dynamic_slice(rows, (0, 0, ROWS + 2 + expert // 8, at), (4, 2, 1, ROWS))
    return (high.astype(F32) + low.astype(F32)).reshape(8, ROWS)


def attention_kernel(place, q_ref, kv_ref, qseg_ref, out_ref, kcat, bias):
    z, hi, y, c = place[0], place[1], place[2], place[3]
    qpos = (hi * Z + z) * ROWS + lax.broadcasted_iota(jnp.int32, (ROWS, ROWS), 0)
    lane = lax.broadcasted_iota(jnp.int32, (ROWS, ROWS), 1)
    qseg = qseg_ref[...]
    for j in range(9):
        if j < 8:
            upper = (z < j).astype(jnp.int32)
            at = j * (2 * PART) + (1 - upper) * PART
            first = jnp.where(
                upper == 1, jnp.where(hi == 1, j * ROWS, 1 << 20), (hi * Z + j) * ROWS
            )
        else:
            at = z * (2 * PART)
            first = jnp.where(hi == 1, z * ROWS, 1 << 20)
        at = pl.multiple_of(at, 16)
        kcat[pl.ds(j * ROWS, ROWS), :] = kv_ref[pl.ds(at, ROWS), :]
        kseg = kv_ref[pl.ds(pl.multiple_of(at + ROWS, 16), SEG_ROWS), 0:ROWS].astype(F32)[0:1, :]
        visible = (first + lane <= qpos) & (kseg == qseg)
        bias[:, pl.ds(j * ROWS, ROWS)] = jnp.where(visible, F32(0.0), F32(MASKED))
    scale = HEAD_DIM ** (-0.5)
    for rel in range(2):
        for yy in range(2):
            kvh = lax.rem(y + yy, 2)
            base = kvh * 8 + lax.rem(c + rel, 2)
            qs = jnp.concatenate(
                [
                    q_ref[:, pl.ds(pl.multiple_of((base + 2 * x) * HEAD_DIM, 128), HEAD_DIM)]
                    for x in range(4)
                ],
                axis=0,
            )
            k = kcat[:, pl.ds(pl.multiple_of(kvh * HEAD_DIM, 128), HEAD_DIM)]
            v = kcat[:, pl.ds(pl.multiple_of(256 + kvh * HEAD_DIM, 128), HEAD_DIM)]
            s = lax.dot_general(qs, k, (((1,), (1,)), ((), ())), preferred_element_type=F32)
            s = s.reshape(4, ROWS, KEYS) * scale + bias[...][None]
            top = jnp.max(s, axis=-1, keepdims=True)
            w = jnp.exp(s - top)
            total = jnp.sum(w, axis=-1, keepdims=True).reshape(4 * ROWS, 1)
            a = jnp.dot(
                w.astype(BF16).reshape(4 * ROWS, KEYS), v, preferred_element_type=F32
            )
            a = (a / total).astype(BF16)
            for x in range(4):
                out_ref[:, pl.ds(rel * HALF + (2 * x + yy) * HEAD_DIM, HEAD_DIM)] = a[
                    x * ROWS : (x + 1) * ROWS
                ]


def attention(place, q, kv, qseg):
    return pl.pallas_call(
        attention_kernel,
        out_shape=jax.ShapeDtypeStruct((ROWS, D), BF16),
        in_specs=[SM, VM, VM, VM],
        out_specs=VM,
        scratch_shapes=[pltpu.VMEM((KEYS, 512), BF16), pltpu.VMEM((ROWS, KEYS), F32)],
        compiler_params=params(24),
        cost_estimate=pl.CostEstimate(
            flops=4 * HEADS * ROWS * KEYS * HEAD_DIM,
            bytes_accessed=4 << 20,
            transcendentals=HEADS * ROWS * KEYS,
        ),
    )(place, q, kv, qseg)


def right_rows(x_ref, y_ref):
    parts = []
    for x in range(4):
        parts += [x_ref[x], y_ref[x]]
    return jnp.concatenate(parts, axis=0)


def project_kernel(
    att_ref, fo, sox, soy, fx, sxx, sxy, res_ref, gain_ref, hid_ref, first_ref, second_ref
):
    own, other = att_ref[:, :HALF], att_ref[:, HALF:]
    fo_rows = fo[:, :, 0:ROWS, :].reshape(HALF, HALF)
    fx_rows = fx[:, :, 0:ROWS, :].reshape(HALF, HALF)
    left = jnp.dot(own, fo_rows, preferred_element_type=F32) + jnp.dot(
        other, fx_rows, preferred_element_type=F32
    )
    right = jnp.dot(own, right_rows(sox, soy), preferred_element_type=F32) + jnp.dot(
        other, right_rows(sxx, sxy), preferred_element_type=F32
    )
    left = left + res_ref[:, :HALF].astype(F32)
    right = right + res_ref[:, HALF:].astype(F32)
    hid_ref[:, :HALF] = left
    hid_ref[:, HALF:] = right
    square = jnp.sum(left * left, axis=-1, keepdims=True) + jnp.sum(
        right * right, axis=-1, keepdims=True
    )
    scale = lax.rsqrt(square * (1.0 / D) + 1e-06)
    gain = gain_ref[...]
    first_ref[...] = (left * scale * gain[:, :HALF]).astype(BF16)
    second = (right * scale * gain[:, HALF:]).astype(BF16)
    for x in range(4):
        second_ref[x] = second


def project(att, own, other, residual, gain):
    return pl.pallas_call(
        project_kernel,
        out_shape=(
            jax.ShapeDtypeStruct((ROWS, D), F32),
            jax.ShapeDtypeStruct((ROWS, HALF), BF16),
            jax.ShapeDtypeStruct((4, ROWS, HALF), BF16),
        ),
        in_specs=[VM] * 9,
        out_specs=(VM, VM, VM),
        compiler_params=params(54),
        cost_estimate=pl.CostEstimate(
            flops=2 * ROWS * D * D, bytes_accessed=11 << 20, transcendentals=ROWS
        ),
    )(att, *own, *other, residual, gain)


def pick_rows(gates):
    named = (gates > 0.0).astype(F32)
    before = (
        lax.broadcasted_iota(jnp.int32, (ROWS, ROWS), 0)
        < lax.broadcasted_iota(jnp.int32, (ROWS, ROWS), 1)
    ).astype(BF16)
    rank = jnp.dot(named.astype(BF16), before, preferred_element_type=F32)
    rank = jnp.where(named > 0.5, rank, F32(-1.0))
    row = lax.broadcasted_iota(jnp.int32, (2 * CAP, 2 * ROWS), 0)
    lane = lax.broadcasted_iota(jnp.int32, (2 * CAP, 2 * ROWS), 1)
    second = row >= CAP
    slot = jnp.where(second, row - CAP, row)
    slot = jnp.where(second == (lane >= ROWS), slot, -2).astype(F32)
    picks, scales = [], []
    for x in range(4):
        both = jnp.concatenate([rank[2 * x : 2 * x + 1], rank[2 * x + 1 : 2 * x + 2]], axis=1)
        here = (both == slot).astype(F32)
        gate = jnp.concatenate([gates[2 * x : 2 * x + 1], gates[2 * x + 1 : 2 * x + 2]], axis=1)
        scales.append(jnp.sum(here * gate, axis=1, keepdims=True))
        picks.append(here.astype(BF16))
    return picks, scales


def activate(picks, a_ref, bx_ref, by_ref, g_ref, u_ref, rows):
    for x in range(4):
        left = jnp.dot(picks[x], a_ref[x].reshape(2 * ROWS, HALF), preferred_element_type=F32)
        tokens = jnp.concatenate([bx_ref[x], by_ref[x]], axis=0)
        right = jnp.dot(picks[x], tokens, preferred_element_type=F32)
        rows[pl.ds(x * 2 * CAP, 2 * CAP), :HALF] = left.astype(BF16)
        rows[pl.ds(x * 2 * CAP, 2 * CAP), HALF:] = right.astype(BF16)
    gate = jnp.dot(rows[...], g_ref[...], preferred_element_type=F32)
    up = jnp.dot(rows[...], u_ref[...], preferred_element_type=F32)
    return (gate / (1.0 + jnp.exp(-gate)) * up).astype(BF16)


def gated_blocks(x, side, picks, scales, activ_ref, d_ref):
    rows = activ_ref[pl.ds(x * 2 * CAP, 2 * CAP), :]
    o = jnp.dot(rows, d_ref[:, pl.ds(side * HALF, HALF)], preferred_element_type=F32)
    o = (o * scales[x]).astype(BF16)
    return lax.dot_general(picks[x], o, (((0,), (0,)), ((), ())), preferred_element_type=F32)


def down_blocks(side, picks, scales, activ_ref, d_ref, out_ref):
    for x in range(4):
        dense = gated_blocks(x, side, picks, scales, activ_ref, d_ref).astype(BF16)
        out_ref[x] = dense.reshape(2, ROWS, HALF)


def up_kernel(a_ref, bx_ref, by_ref, gate_ref, g_ref, u_ref, out_ref, rows):
    picks, _ = pick_rows(gate_ref[...])
    out_ref[...] = activate(picks, a_ref, bx_ref, by_ref, g_ref, u_ref, rows)


def up_down_kernel(
    a_ref, bx_ref, by_ref, gate_ref, g_ref, u_ref, d_ref, activ_ref, out_ref, rows
):
    picks, scales = pick_rows(gate_ref[...])
    activ_ref[...] = activate(picks, a_ref, bx_ref, by_ref, g_ref, u_ref, rows)
    down_blocks(1, picks, scales, activ_ref, d_ref, out_ref)


def down_first_kernel(activ_ref, gate_ref, d_ref, out_ref):
    picks, scales = pick_rows(gate_ref[...])
    down_blocks(0, picks, scales, activ_ref, d_ref, out_ref)


def add_second_kernel(activ_ref, gate_ref, d_ref, add_ref, out_ref):
    picks, scales = pick_rows(gate_ref[...])
    for x in range(4):
        dense = gated_blocks(x, 1, picks, scales, activ_ref, d_ref)
        out_ref[x] = (dense.reshape(2, ROWS, HALF) + add_ref[x].astype(F32)).astype(BF16)


def add_first_kernel(activ_ref, gate_ref, d_ref, add_ref, keep_ref, send_ref):
    picks, scales = pick_rows(gate_ref[...])
    for x in range(4):
        dense = gated_blocks(x, 0, picks, scales, activ_ref, d_ref)
        keep_ref[x] = (dense[:ROWS] + add_ref[x, 0].astype(F32)).astype(BF16)
        send_ref[x] = (dense[ROWS:] + add_ref[x, 1].astype(F32)).astype(BF16)


PICKED = SLOTS // 2
ROW_SCRATCH = pltpu.VMEM((PICKED, D), BF16)


def kernel_call(body, out_shape, mib, flops, moved, scratch=()):
    many = isinstance(out_shape, tuple)

    def call(*operands):
        return pl.pallas_call(
            body,
            out_shape=out_shape,
            in_specs=[VM] * len(operands),
            out_specs=(VM,) * len(out_shape) if many else VM,
            scratch_shapes=scratch,
            compiler_params=params(mib),
            cost_estimate=pl.CostEstimate(flops=flops, bytes_accessed=moved, transcendentals=0),
        )(*operands)

    return call


def shape(*dims, dtype=BF16):
    return jax.ShapeDtypeStruct(dims, dtype)


WHOLE = shape(4, 2, ROWS, HALF)
PART_ROWS = shape(4, ROWS, HALF)
ACTIV = shape(PICKED, FF)
UP_FLOPS = 4 * PICKED * D * FF
DOWN_FLOPS = PICKED * D * FF


def final_kernel(hid_ref, x_ref, b_ref, y_ref, out_ref):
    left = hid_ref[:, :HALF]
    for x in range(4):
        left = left + x_ref[x].astype(F32)
    out_ref[:, :HALF] = left.astype(BF16)
    right = hid_ref[:, HALF:] + (b_ref[...] + y_ref[...].astype(F32))
    out_ref[:, HALF:] = right.astype(BF16)


def touch_kernel(g_ref, u_ref, d_ref, after_ref, out_ref):
    out_ref[...] = after_ref[...]


def touch(matrices, after):
    return kernel_call(touch_kernel, shape(*after.shape, dtype=F32), 4, 0, 20 << 20)(
        *matrices, after
    )


def spread_tokens(first, second):
    first_y = y_swap(first)
    second_x = x_exchange(second)
    first_y, second_x = lax.optimization_barrier((first_y, second_x))
    second_y = y_swap(second_x)
    pair = jnp.stack([first, first_y])
    first_all = x_spread(pair)
    own = (first_all, second_x, second_y)
    return own, pair


def reduce_back(keep, send, both, hidden):
    got_y = y_swap(send)
    got_x = x_exchange(both)
    part_a = (keep.astype(F32) + got_y.astype(F32)).astype(BF16)
    part_b = jnp.sum(got_x.astype(F32), axis=0)
    last_y = y_swap(part_b[1].astype(BF16))
    last_x = x_exchange(part_a)
    return kernel_call(final_kernel, shape(ROWS, D), 12, ROWS * D, 4 << 20)(
        hidden, last_x, part_b[0], last_y
    )


def per_device(
    queries,
    keys,
    values,
    segments,
    residual,
    out_weight,
    norm_gain,
    expert_ids,
    gate_weights,
    w_gate,
    w_up,
    w_down,
):
    ctx, exp = lax.axis_index("ctx"), lax.axis_index("exp")
    place = jnp.stack([ctx % Z, ctx // Z, exp // 8, exp % 2]).astype(jnp.int32)
    seg_rows = jnp.broadcast_to(
        jnp.pad(segments.astype(BF16), ((0, 0), (0, 512 - ROWS))), (SEG_ROWS, 512)
    )
    own = jnp.concatenate(
        [jnp.concatenate([keys[0], values[0]], axis=1), seg_rows], axis=0
    )
    upper = lax.ppermute(own, "ctx", [(s, s + Z) for s in range(Z)])
    kv = lax.all_gather(
        jnp.concatenate([upper, own], axis=0),
        "ctx",
        axis=0,
        tiled=True,
        axis_index_groups=Z_GROUPS,
    )
    weight, weight_other = gather_weight(
        out_weight, gate_rows(expert_ids[0], gate_weights[0])
    )
    att = attention(place, queries[0], kv, segments[0].astype(F32)[:, None])
    hidden, first, second = project(att, weight, weight_other, residual[0], norm_gain[None, :])
    own, pair = spread_tokens(first, second)
    gates, gates_other = own_gates(weight[0], exp), own_gates(weight_other[0], exp)
    matrices = (w_gate[0], w_up[0], w_down[0])
    gates_other, _ = lax.optimization_barrier((gates_other, pair))
    gates_other = touch(matrices, gates_other)
    other = tuple(swap(v) for v in own)
    activ = kernel_call(up_kernel, ACTIV, 24, UP_FLOPS, 10 << 20, [ROW_SCRATCH])(
        *own, gates, *matrices[:2]
    )
    activ_other, second = kernel_call(
        up_down_kernel, (ACTIV, WHOLE), 24, UP_FLOPS + DOWN_FLOPS, 12 << 20, [ROW_SCRATCH]
    )(*other, gates_other, *matrices)
    add_second = swap(second)
    first = kernel_call(down_first_kernel, WHOLE, 16, DOWN_FLOPS, 5 << 20)(
        activ_other, gates_other, matrices[2]
    )
    add_first = swap(first)
    both = kernel_call(add_second_kernel, WHOLE, 16, DOWN_FLOPS, 7 << 20)(
        activ, gates, matrices[2], add_second
    )
    keep, send = kernel_call(
        add_first_kernel, (PART_ROWS, PART_ROWS), 16, DOWN_FLOPS, 7 << 20
    )(activ, gates, matrices[2], add_first)
    return reduce_back(keep, send, both, hidden)[None]


def solution(mesh):
    return jax.shard_map(
        per_device,
        mesh=mesh,
        in_specs=(
            P("exp", "ctx", None),
            P("exp", "ctx", None),
            P("exp", "ctx", None),
            P("exp", "ctx"),
            P("exp", "ctx", None),
            P("exp", None),
            P(),
            P("exp", "ctx", None),
            P("exp", "ctx", None),
            P("exp", None, None),
            P("exp", None, None),
            P("exp", None, None),
        ),
        out_specs=P("exp", "ctx", None),
        check_vma=False,
    )
```

```python
import functools

import jax
import jax.numpy as jnp
from jax import lax
from jax.experimental import pallas as pl
from jax.experimental.pallas import tpu as pltpu
from jax.sharding import PartitionSpec as P

D = 2048
HEADS = 16
HEAD_DIM = 128
ROWS = 128
EXPERTS = 16
CAP = 72
SLOTS = EXPERTS * CAP
FF = 768
HALF = D // 2
Z = 8
SEG_ROWS = 16
PART = ROWS + SEG_ROWS
KEYS = 9 * ROWS
MASKED = -1e30
BF16 = jnp.bfloat16
F32 = jnp.float32

VM = pl.BlockSpec(memory_space=pltpu.VMEM)
SM = pl.BlockSpec(memory_space=pltpu.SMEM)


def params(mib, **kw):
    return pltpu.CompilerParams(vmem_limit_bytes=mib << 20, **kw)


def exp_pairs(f):
    pairs = []
    for e in range(16):
        y, x, c = f(e // 8, (e // 2) % 4, e % 2)
        pairs.append((e, (y % 2) * 8 + (x % 4) * 2 + c % 2))
    return pairs


CORE_SWAP = exp_pairs(lambda y, x, c: (y, x, c + 1))
Y_SWAP = exp_pairs(lambda y, x, c: (y + 1, x, c))
X_GROUPS = [[y * 8 + x * 2 + c for x in range(4)] for y in range(2) for c in range(2)]
Z_GROUPS = [list(range(8)), list(range(8, 16))]


def swap(v):
    return lax.ppermute(v, "exp", CORE_SWAP)


def y_swap(v):
    return lax.ppermute(v, "exp", Y_SWAP)


def x_exchange(v):
    return lax.all_to_all(
        v, "exp", split_axis=0, concat_axis=0, tiled=True, axis_index_groups=X_GROUPS
    )


def x_spread(v):
    return x_exchange(jnp.broadcast_to(v[None], (4,) + v.shape))


def gather_weight(w, extra, after):
    first = jnp.concatenate([w[:, :HALF], extra], axis=0)
    first, after = lax.optimization_barrier((first, after))
    first_y = y_swap(first)
    second_x = x_spread(w[:, HALF:])
    first_y, second_x = lax.optimization_barrier((first_y, second_x))
    second_y = y_swap(second_x)
    first_all = x_spread(jnp.stack([first, first_y]))
    second_x_other = swap(second_x)
    first_all, second_y, second_x_other = lax.optimization_barrier(
        (first_all, second_y, second_x_other)
    )
    own = (first_all, second_x, second_y)
    return own, (swap(first_all), second_x_other, swap(second_y)), after


def gate_rows(ids, gates):
    same = ids[None, :, :] == jnp.arange(EXPERTS, dtype=jnp.int32)[:, None, None]
    table = jnp.sum(jnp.where(same, gates[None], 0.0), axis=2)
    high = table.astype(BF16)
    low = (table - high.astype(F32)).astype(BF16)
    flat = jnp.concatenate([high.reshape(2, HALF), low.reshape(2, HALF)], axis=0)
    return jnp.pad(flat, ((0, 4), (0, 0)))


def own_gates(rows, expert):
    at = (expert % 8) * ROWS
    high = lax.dynamic_slice(rows, (0, 0, ROWS + expert // 8, at), (4, 2, 1, ROWS))
    low = lax.dynamic_slice(rows, (0, 0, ROWS + 2 + expert // 8, at), (4, 2, 1, ROWS))
    return (high.astype(F32) + low.astype(F32)).reshape(8, ROWS)


def attention_kernel(place, q_ref, kv_ref, qseg_ref, out_ref, kcat, bias):
    z, hi, y, c = place[0], place[1], place[2], place[3]
    qpos = (hi * Z + z) * ROWS + lax.broadcasted_iota(jnp.int32, (ROWS, ROWS), 0)
    lane = lax.broadcasted_iota(jnp.int32, (ROWS, ROWS), 1)
    qseg = qseg_ref[...]
    for j in range(9):
        if j < 8:
            upper = (z < j).astype(jnp.int32)
            at = j * (2 * PART) + (1 - upper) * PART
            first = jnp.where(
                upper == 1, jnp.where(hi == 1, j * ROWS, 1 << 20), (hi * Z + j) * ROWS
            )
        else:
            at = z * (2 * PART)
            first = jnp.where(hi == 1, z * ROWS, 1 << 20)
        at = pl.multiple_of(at, 16)
        kcat[pl.ds(j * ROWS, ROWS), :] = kv_ref[pl.ds(at, ROWS), :]
        kseg = kv_ref[pl.ds(pl.multiple_of(at + ROWS, 16), SEG_ROWS), 0:ROWS].astype(F32)[0:1, :]
        visible = (first + lane <= qpos) & (kseg == qseg)
        bias[:, pl.ds(j * ROWS, ROWS)] = jnp.where(visible, F32(0.0), F32(MASKED))
    scale = HEAD_DIM ** (-0.5)
    for rel in range(2):
        for yy in range(2):
            kvh = lax.rem(y + yy, 2)
            base = kvh * 8 + lax.rem(c + rel, 2)
            qs = jnp.concatenate(
                [
                    q_ref[:, pl.ds(pl.multiple_of((base + 2 * x) * HEAD_DIM, 128), HEAD_DIM)]
                    for x in range(4)
                ],
                axis=0,
            )
            k = kcat[:, pl.ds(pl.multiple_of(kvh * HEAD_DIM, 128), HEAD_DIM)]
            v = kcat[:, pl.ds(pl.multiple_of(256 + kvh * HEAD_DIM, 128), HEAD_DIM)]
            s = lax.dot_general(qs, k, (((1,), (1,)), ((), ())), preferred_element_type=F32)
            s = s.reshape(4, ROWS, KEYS) * scale + bias[...][None]
            top = jnp.max(s, axis=-1, keepdims=True)
            w = jnp.exp(s - top)
            total = jnp.sum(w, axis=-1, keepdims=True).reshape(4 * ROWS, 1)
            a = jnp.dot(
                w.astype(BF16).reshape(4 * ROWS, KEYS), v, preferred_element_type=F32
            )
            a = (a / total).astype(BF16)
            for x in range(4):
                out_ref[:, pl.ds(rel * HALF + (2 * x + yy) * HEAD_DIM, HEAD_DIM)] = a[
                    x * ROWS : (x + 1) * ROWS
                ]


def attention(place, q, kv, qseg):
    return pl.pallas_call(
        attention_kernel,
        out_shape=jax.ShapeDtypeStruct((ROWS, D), BF16),
        in_specs=[SM, VM, VM, VM],
        out_specs=VM,
        scratch_shapes=[pltpu.VMEM((KEYS, 512), BF16), pltpu.VMEM((ROWS, KEYS), F32)],
        compiler_params=params(24),
        cost_estimate=pl.CostEstimate(
            flops=4 * HEADS * ROWS * KEYS * HEAD_DIM,
            bytes_accessed=4 << 20,
            transcendentals=HEADS * ROWS * KEYS,
        ),
    )(place, q, kv, qseg)


def right_rows(x_ref, y_ref):
    parts = []
    for x in range(4):
        parts += [x_ref[x], y_ref[x]]
    return jnp.concatenate(parts, axis=0)


def project_kernel(
    att_ref, fo, sox, soy, fx, sxx, sxy, res_ref, gain_ref, hid_ref, first_ref, second_ref
):
    own, other = att_ref[:, :HALF], att_ref[:, HALF:]
    fo_rows = fo[:, :, 0:ROWS, :].reshape(HALF, HALF)
    fx_rows = fx[:, :, 0:ROWS, :].reshape(HALF, HALF)
    left = jnp.dot(own, fo_rows, preferred_element_type=F32) + jnp.dot(
        other, fx_rows, preferred_element_type=F32
    )
    right = jnp.dot(own, right_rows(sox, soy), preferred_element_type=F32) + jnp.dot(
        other, right_rows(sxx, sxy), preferred_element_type=F32
    )
    left = left + res_ref[:, :HALF].astype(F32)
    right = right + res_ref[:, HALF:].astype(F32)
    hid_ref[:, :HALF] = left
    hid_ref[:, HALF:] = right
    square = jnp.sum(left * left, axis=-1, keepdims=True) + jnp.sum(
        right * right, axis=-1, keepdims=True
    )
    scale = lax.rsqrt(square * (1.0 / D) + 1e-06)
    gain = gain_ref[...]
    first_ref[...] = (left * scale * gain[:, :HALF]).astype(BF16)
    second = (right * scale * gain[:, HALF:]).astype(BF16)
    for x in range(4):
        second_ref[x] = second


def project(att, own, other, residual, gain):
    return pl.pallas_call(
        project_kernel,
        out_shape=(
            jax.ShapeDtypeStruct((ROWS, D), F32),
            jax.ShapeDtypeStruct((ROWS, HALF), BF16),
            jax.ShapeDtypeStruct((4, ROWS, HALF), BF16),
        ),
        in_specs=[VM] * 9,
        out_specs=(VM, VM, VM),
        compiler_params=params(50),
        cost_estimate=pl.CostEstimate(
            flops=2 * ROWS * D * D, bytes_accessed=11 << 20, transcendentals=ROWS
        ),
    )(att, *own, *other, residual, gain)


def pick_rows(gates):
    named = (gates > 0.0).astype(F32)
    before = (
        lax.broadcasted_iota(jnp.int32, (ROWS, ROWS), 0)
        < lax.broadcasted_iota(jnp.int32, (ROWS, ROWS), 1)
    ).astype(BF16)
    rank = jnp.dot(named.astype(BF16), before, preferred_element_type=F32)
    rank = jnp.where(named > 0.5, rank, F32(-1.0))
    row = lax.broadcasted_iota(jnp.int32, (2 * CAP, 2 * ROWS), 0)
    lane = lax.broadcasted_iota(jnp.int32, (2 * CAP, 2 * ROWS), 1)
    second = row >= CAP
    slot = jnp.where(second, row - CAP, row)
    slot = jnp.where(second == (lane >= ROWS), slot, -2).astype(F32)
    picks, scales = [], []
    for x in range(4):
        both = jnp.concatenate([rank[2 * x : 2 * x + 1], rank[2 * x + 1 : 2 * x + 2]], axis=1)
        here = (both == slot).astype(F32)
        gate = jnp.concatenate([gates[2 * x : 2 * x + 1], gates[2 * x + 1 : 2 * x + 2]], axis=1)
        scales.append(jnp.sum(here * gate, axis=1, keepdims=True))
        picks.append(here.astype(BF16))
    return picks, scales


def activate(picks, a_ref, bx_ref, by_ref, g_ref, u_ref, rows):
    for x in range(4):
        left = jnp.dot(picks[x], a_ref[x].reshape(2 * ROWS, HALF), preferred_element_type=F32)
        tokens = jnp.concatenate([bx_ref[x], by_ref[x]], axis=0)
        right = jnp.dot(picks[x], tokens, preferred_element_type=F32)
        rows[pl.ds(x * 2 * CAP, 2 * CAP), :HALF] = left.astype(BF16)
        rows[pl.ds(x * 2 * CAP, 2 * CAP), HALF:] = right.astype(BF16)
    gate = jnp.dot(rows[...], g_ref[...], preferred_element_type=F32)
    up = jnp.dot(rows[...], u_ref[...], preferred_element_type=F32)
    return (gate / (1.0 + jnp.exp(-gate)) * up).astype(BF16)


def gated_blocks(x, picks, scales, activ, d_ref):
    o = jnp.dot(activ[x * 2 * CAP : (x + 1) * 2 * CAP], d_ref[...], preferred_element_type=F32)
    o = (o * scales[x]).astype(BF16)
    return lax.dot_general(picks[x], o, (((0,), (0,)), ((), ())), preferred_element_type=F32)


def other_kernel(a_ref, bx_ref, by_ref, gate_ref, g_ref, u_ref, d_ref, out_ref, rows):
    picks, scales = pick_rows(gate_ref[...])
    activ = activate(picks, a_ref, bx_ref, by_ref, g_ref, u_ref, rows)
    for x in range(4):
        dense = gated_blocks(x, picks, scales, activ, d_ref).astype(BF16)
        for yy in range(2):
            out_ref[0, x, yy] = dense[yy * ROWS : (yy + 1) * ROWS, :HALF]
            out_ref[1, x, yy] = dense[yy * ROWS : (yy + 1) * ROWS, HALF:]


def own_up_kernel(a_ref, bx_ref, by_ref, gate_ref, g_ref, u_ref, out_ref, rows):
    picks, _ = pick_rows(gate_ref[...])
    out_ref[...] = activate(picks, a_ref, bx_ref, by_ref, g_ref, u_ref, rows)


def own_down_kernel(activ_ref, gate_ref, d_ref, add_ref, keep_ref, send_ref, both_ref):
    picks, scales = pick_rows(gate_ref[...])
    activ = activ_ref[...]
    for x in range(4):
        dense = gated_blocks(x, picks, scales, activ, d_ref)
        for yy in range(2):
            d = dense[yy * ROWS : (yy + 1) * ROWS]
            part = (d[:, :HALF] + add_ref[0, x, yy].astype(F32)).astype(BF16)
            (send_ref if yy else keep_ref)[x] = part
            both_ref[x, yy] = (d[:, HALF:] + add_ref[1, x, yy].astype(F32)).astype(BF16)


PICKED = SLOTS // 2
ROW_SCRATCH = pltpu.VMEM((PICKED, D), BF16)


def kernel_call(body, out_shape, mib, flops, moved, scratch=()):
    many = isinstance(out_shape, tuple)

    def call(*operands):
        return pl.pallas_call(
            body,
            out_shape=out_shape,
            in_specs=[VM] * len(operands),
            out_specs=(VM,) * len(out_shape) if many else VM,
            scratch_shapes=scratch,
            compiler_params=params(mib),
            cost_estimate=pl.CostEstimate(flops=flops, bytes_accessed=moved, transcendentals=0),
        )(*operands)

    return call


def shape(*dims, dtype=BF16):
    return jax.ShapeDtypeStruct(dims, dtype)


def experts_other(tokens, gates, w_gate, w_up, w_down):
    return kernel_call(
        other_kernel,
        shape(2, 4, 2, ROWS, HALF),
        24,
        6 * PICKED * D * FF,
        16 << 20,
        [ROW_SCRATCH],
    )(*tokens, gates, w_gate, w_up, w_down)


def experts_own_up(tokens, gates, w_gate, w_up):
    return kernel_call(
        own_up_kernel, shape(PICKED, FF), 24, 4 * PICKED * D * FF, 10 << 20, [ROW_SCRATCH]
    )(*tokens, gates, w_gate, w_up)


def experts_own_down(activ, gates, w_down, add):
    return kernel_call(
        own_down_kernel,
        (shape(4, ROWS, HALF), shape(4, ROWS, HALF), shape(4, 2, ROWS, HALF)),
        36,
        2 * PICKED * D * FF,
        12 << 20,
    )(activ, gates, w_down, add)


def final_kernel(hid_ref, x_ref, b_ref, y_ref, out_ref):
    left = hid_ref[:, :HALF]
    for x in range(4):
        left = left + x_ref[x].astype(F32)
    out_ref[:, :HALF] = left.astype(BF16)
    right = hid_ref[:, HALF:] + (b_ref[...] + y_ref[...].astype(F32))
    out_ref[:, HALF:] = right.astype(BF16)


def touch_kernel(g_ref, u_ref, d_ref, after_ref, out_ref):
    out_ref[...] = after_ref[...]


def touch(matrices, after):
    return kernel_call(touch_kernel, shape(*after.shape, dtype=F32), 4, 0, 20 << 20)(
        *matrices, after
    )


def spread_tokens(first, second, gates, gates_other, matrices):
    first_y = y_swap(first)
    second_x = x_exchange(second)
    first_y, second_x, gates, gates_other = lax.optimization_barrier(
        (first_y, second_x, gates, gates_other)
    )
    second_y = y_swap(second_x)
    first_all = x_spread(jnp.stack([first, first_y]))
    second_x_other = swap(second_x)
    first_all, second_x_other, gates_other = lax.optimization_barrier(
        (first_all, second_x_other, gates_other)
    )
    gates_other = touch(matrices, gates_other)
    own = (first_all, second_x, second_y)
    return own, (swap(first_all), second_x_other, swap(second_y)), gates, gates_other


def reduce_back(keep, send, both, hidden):
    got_y = y_swap(send)
    got_x = x_exchange(both)
    part_a = (keep.astype(F32) + got_y.astype(F32)).astype(BF16)
    part_b = jnp.sum(got_x.astype(F32), axis=0)
    last_y = y_swap(part_b[1].astype(BF16))
    last_x = x_exchange(part_a)
    return kernel_call(final_kernel, shape(ROWS, D), 12, ROWS * D, 4 << 20)(
        hidden, last_x, part_b[0], last_y
    )


def per_device(
    queries,
    keys,
    values,
    segments,
    residual,
    out_weight,
    norm_gain,
    expert_ids,
    gate_weights,
    w_gate,
    w_up,
    w_down,
):
    ctx, exp = lax.axis_index("ctx"), lax.axis_index("exp")
    place = jnp.stack([ctx % Z, ctx // Z, exp // 8, exp % 2]).astype(jnp.int32)
    seg_rows = jnp.broadcast_to(
        jnp.pad(segments.astype(BF16), ((0, 0), (0, 512 - ROWS))), (SEG_ROWS, 512)
    )
    own = jnp.concatenate(
        [jnp.concatenate([keys[0], values[0]], axis=1), seg_rows], axis=0
    )
    upper = lax.ppermute(own, "ctx", [(s, s + Z) for s in range(Z)])
    both_levels = jnp.concatenate([upper, own], axis=0)
    weight, weight_other, both_levels = gather_weight(
        out_weight, gate_rows(expert_ids[0], gate_weights[0]), both_levels
    )
    kv = lax.all_gather(both_levels, "ctx", axis=0, tiled=True, axis_index_groups=Z_GROUPS)
    att = attention(place, queries[0], kv, segments[0].astype(F32)[:, None])
    hidden, first, second = project(att, weight, weight_other, residual[0], norm_gain[None, :])
    matrices = (w_gate[0], w_up[0], w_down[0])
    own, other, gates, gates_other = spread_tokens(
        first, second, own_gates(weight[0], exp), own_gates(weight_other[0], exp), matrices
    )
    partial = swap(experts_other(other, gates_other, *matrices))
    activ = experts_own_up(own, gates, *matrices[:2])
    keep, send, both = experts_own_down(activ, gates, matrices[2], partial)
    return reduce_back(keep, send, both, hidden)[None]


def solution(mesh):
    return jax.shard_map(
        per_device,
        mesh=mesh,
        in_specs=(
            P("exp", "ctx", None),
            P("exp", "ctx", None),
            P("exp", "ctx", None),
            P("exp", "ctx"),
            P("exp", "ctx", None),
            P("exp", None),
            P(),
            P("exp", "ctx", None),
            P("exp", "ctx", None),
            P("exp", None, None),
            P("exp", None, None),
            P("exp", None, None),
        ),
        out_specs=P("exp", "ctx", None),
        check_vma=False,
    )
```

```python
import functools

import jax
import jax.numpy as jnp
from jax import lax
from jax.experimental import pallas as pl
from jax.experimental.pallas import tpu as pltpu
from jax.sharding import PartitionSpec as P

D = 2048
HEADS = 16
HEAD_DIM = 128
ROWS = 128
EXPERTS = 16
CAP = 72
SLOTS = EXPERTS * CAP
FF = 768
HALF = D // 2
Z = 8
SEG_ROWS = 16
PART = ROWS + SEG_ROWS
KEYS = 9 * ROWS
MASKED = -1e30
BF16 = jnp.bfloat16
F32 = jnp.float32

VM = pl.BlockSpec(memory_space=pltpu.VMEM)
SM = pl.BlockSpec(memory_space=pltpu.SMEM)


def params(mib, **kw):
    return pltpu.CompilerParams(vmem_limit_bytes=mib << 20, **kw)


def exp_pairs(f):
    pairs = []
    for e in range(16):
        y, x, c = f(e // 8, (e // 2) % 4, e % 2)
        pairs.append((e, (y % 2) * 8 + (x % 4) * 2 + c % 2))
    return pairs


CORE_SWAP = exp_pairs(lambda y, x, c: (y, x, c + 1))
Y_SWAP = exp_pairs(lambda y, x, c: (y + 1, x, c))
X_GROUPS = [[y * 8 + x * 2 + c for x in range(4)] for y in range(2) for c in range(2)]
Z_GROUPS = [list(range(8)), list(range(8, 16))]


def swap(v):
    return lax.ppermute(v, "exp", CORE_SWAP)


def y_swap(v):
    return lax.ppermute(v, "exp", Y_SWAP)


def x_exchange(v):
    return lax.all_to_all(
        v, "exp", split_axis=0, concat_axis=0, tiled=True, axis_index_groups=X_GROUPS
    )


def x_spread(v):
    return x_exchange(jnp.broadcast_to(v[None], (4,) + v.shape))


def gather_weight(w, extra, after):
    first = jnp.concatenate([w[:, :HALF], extra], axis=0)
    first, after = lax.optimization_barrier((first, after))
    first_y = y_swap(first)
    second_x = x_spread(w[:, HALF:])
    first_y, second_x = lax.optimization_barrier((first_y, second_x))
    second_y = y_swap(second_x)
    first_all = x_spread(jnp.stack([first, first_y]))
    second_x_other = swap(second_x)
    first_all, second_y, second_x_other = lax.optimization_barrier(
        (first_all, second_y, second_x_other)
    )
    own = (first_all, second_x, second_y)
    return own, (swap(first_all), second_x_other, swap(second_y)), after


def gate_rows(ids, gates):
    same = ids[None, :, :] == jnp.arange(EXPERTS, dtype=jnp.int32)[:, None, None]
    table = jnp.sum(jnp.where(same, gates[None], 0.0), axis=2)
    high = table.astype(BF16)
    low = (table - high.astype(F32)).astype(BF16)
    flat = jnp.concatenate([high.reshape(2, HALF), low.reshape(2, HALF)], axis=0)
    return jnp.pad(flat, ((0, 4), (0, 0)))


def own_gates(rows, expert):
    at = (expert % 8) * ROWS
    high = lax.dynamic_slice(rows, (0, 0, ROWS + expert // 8, at), (4, 2, 1, ROWS))
    low = lax.dynamic_slice(rows, (0, 0, ROWS + 2 + expert // 8, at), (4, 2, 1, ROWS))
    return (high.astype(F32) + low.astype(F32)).reshape(8, ROWS)


def attention_kernel(place, q_ref, kv_ref, qseg_ref, out_ref, kcat, bias):
    z, hi, y, c = place[0], place[1], place[2], place[3]
    qpos = (hi * Z + z) * ROWS + lax.broadcasted_iota(jnp.int32, (ROWS, ROWS), 0)
    lane = lax.broadcasted_iota(jnp.int32, (ROWS, ROWS), 1)
    qseg = qseg_ref[...]
    for j in range(9):
        if j < 8:
            upper = (z < j).astype(jnp.int32)
            at = j * (2 * PART) + (1 - upper) * PART
            first = jnp.where(
                upper == 1, jnp.where(hi == 1, j * ROWS, 1 << 20), (hi * Z + j) * ROWS
            )
        else:
            at = z * (2 * PART)
            first = jnp.where(hi == 1, z * ROWS, 1 << 20)
        at = pl.multiple_of(at, 16)
        kcat[pl.ds(j * ROWS, ROWS), :] = kv_ref[pl.ds(at, ROWS), :]
        kseg = kv_ref[pl.ds(pl.multiple_of(at + ROWS, 16), SEG_ROWS), 0:ROWS].astype(F32)[0:1, :]
        visible = (first + lane <= qpos) & (kseg == qseg)
        bias[:, pl.ds(j * ROWS, ROWS)] = jnp.where(visible, F32(0.0), F32(MASKED))
    scale = HEAD_DIM ** (-0.5)
    for rel in range(2):
        for yy in range(2):
            kvh = lax.rem(y + yy, 2)
            base = kvh * 8 + lax.rem(c + rel, 2)
            qs = jnp.concatenate(
                [
                    q_ref[:, pl.ds(pl.multiple_of((base + 2 * x) * HEAD_DIM, 128), HEAD_DIM)]
                    for x in range(4)
                ],
                axis=0,
            )
            k = kcat[:, pl.ds(pl.multiple_of(kvh * HEAD_DIM, 128), HEAD_DIM)]
            v = kcat[:, pl.ds(pl.multiple_of(256 + kvh * HEAD_DIM, 128), HEAD_DIM)]
            s = lax.dot_general(qs, k, (((1,), (1,)), ((), ())), preferred_element_type=F32)
            s = s.reshape(4, ROWS, KEYS) * scale + bias[...][None]
            top = jnp.max(s, axis=-1, keepdims=True)
            w = jnp.exp(s - top)
            total = jnp.sum(w, axis=-1, keepdims=True).reshape(4 * ROWS, 1)
            a = jnp.dot(
                w.astype(BF16).reshape(4 * ROWS, KEYS), v, preferred_element_type=F32
            )
            a = (a / total).astype(BF16)
            for x in range(4):
                out_ref[:, pl.ds(rel * HALF + (2 * x + yy) * HEAD_DIM, HEAD_DIM)] = a[
                    x * ROWS : (x + 1) * ROWS
                ]


def attention(place, q, kv, qseg):
    return pl.pallas_call(
        attention_kernel,
        out_shape=jax.ShapeDtypeStruct((ROWS, D), BF16),
        in_specs=[SM, VM, VM, VM],
        out_specs=VM,
        scratch_shapes=[pltpu.VMEM((KEYS, 512), BF16), pltpu.VMEM((ROWS, KEYS), F32)],
        compiler_params=params(24),
        cost_estimate=pl.CostEstimate(
            flops=4 * HEADS * ROWS * KEYS * HEAD_DIM,
            bytes_accessed=4 << 20,
            transcendentals=HEADS * ROWS * KEYS,
        ),
    )(place, q, kv, qseg)


def right_rows(x_ref, y_ref):
    parts = []
    for x in range(4):
        parts += [x_ref[x], y_ref[x]]
    return jnp.concatenate(parts, axis=0)


def project_kernel(
    att_ref, fo, sox, soy, fx, sxx, sxy, res_ref, gain_ref, hid_ref, first_ref, second_ref
):
    own, other = att_ref[:, :HALF], att_ref[:, HALF:]
    fo_rows = fo[:, :, 0:ROWS, :].reshape(HALF, HALF)
    fx_rows = fx[:, :, 0:ROWS, :].reshape(HALF, HALF)
    left = jnp.dot(own, fo_rows, preferred_element_type=F32) + jnp.dot(
        other, fx_rows, preferred_element_type=F32
    )
    right = jnp.dot(own, right_rows(sox, soy), preferred_element_type=F32) + jnp.dot(
        other, right_rows(sxx, sxy), preferred_element_type=F32
    )
    left = left + res_ref[:, :HALF].astype(F32)
    right = right + res_ref[:, HALF:].astype(F32)
    hid_ref[:, :HALF] = left
    hid_ref[:, HALF:] = right
    square = jnp.sum(left * left, axis=-1, keepdims=True) + jnp.sum(
        right * right, axis=-1, keepdims=True
    )
    scale = lax.rsqrt(square * (1.0 / D) + 1e-06)
    gain = gain_ref[...]
    first_ref[...] = (left * scale * gain[:, :HALF]).astype(BF16)
    second = (right * scale * gain[:, HALF:]).astype(BF16)
    for x in range(4):
        second_ref[x] = second


def project(att, own, other, residual, gain):
    return pl.pallas_call(
        project_kernel,
        out_shape=(
            jax.ShapeDtypeStruct((ROWS, D), F32),
            jax.ShapeDtypeStruct((ROWS, HALF), BF16),
            jax.ShapeDtypeStruct((4, ROWS, HALF), BF16),
        ),
        in_specs=[VM] * 9,
        out_specs=(VM, VM, VM),
        compiler_params=params(50),
        cost_estimate=pl.CostEstimate(
            flops=2 * ROWS * D * D, bytes_accessed=11 << 20, transcendentals=ROWS
        ),
    )(att, *own, *other, residual, gain)


def pick_rows(gates):
    named = (gates > 0.0).astype(F32)
    before = (
        lax.broadcasted_iota(jnp.int32, (ROWS, ROWS), 0)
        < lax.broadcasted_iota(jnp.int32, (ROWS, ROWS), 1)
    ).astype(BF16)
    rank = jnp.dot(named.astype(BF16), before, preferred_element_type=F32)
    rank = jnp.where(named > 0.5, rank, F32(-1.0))
    row = lax.broadcasted_iota(jnp.int32, (2 * CAP, 2 * ROWS), 0)
    lane = lax.broadcasted_iota(jnp.int32, (2 * CAP, 2 * ROWS), 1)
    second = row >= CAP
    slot = jnp.where(second, row - CAP, row)
    slot = jnp.where(second == (lane >= ROWS), slot, -2).astype(F32)
    picks, scales = [], []
    for x in range(4):
        both = jnp.concatenate([rank[2 * x : 2 * x + 1], rank[2 * x + 1 : 2 * x + 2]], axis=1)
        here = (both == slot).astype(F32)
        gate = jnp.concatenate([gates[2 * x : 2 * x + 1], gates[2 * x + 1 : 2 * x + 2]], axis=1)
        scales.append(jnp.sum(here * gate, axis=1, keepdims=True))
        picks.append(here.astype(BF16))
    return picks, scales


def activate(picks, a_ref, bx_ref, by_ref, g_ref, u_ref, rows):
    for x in range(4):
        left = jnp.dot(picks[x], a_ref[x].reshape(2 * ROWS, HALF), preferred_element_type=F32)
        tokens = jnp.concatenate([bx_ref[x], by_ref[x]], axis=0)
        right = jnp.dot(picks[x], tokens, preferred_element_type=F32)
        rows[pl.ds(x * 2 * CAP, 2 * CAP), :HALF] = left.astype(BF16)
        rows[pl.ds(x * 2 * CAP, 2 * CAP), HALF:] = right.astype(BF16)
    gate = jnp.dot(rows[...], g_ref[...], preferred_element_type=F32)
    up = jnp.dot(rows[...], u_ref[...], preferred_element_type=F32)
    return (gate / (1.0 + jnp.exp(-gate)) * up).astype(BF16)


def gated_blocks(x, picks, scales, activ, d_ref):
    o = jnp.dot(activ[x * 2 * CAP : (x + 1) * 2 * CAP], d_ref[...], preferred_element_type=F32)
    o = (o * scales[x]).astype(BF16)
    return lax.dot_general(picks[x], o, (((0,), (0,)), ((), ())), preferred_element_type=F32)


def other_kernel(a_ref, bx_ref, by_ref, gate_ref, g_ref, u_ref, d_ref, out_ref, rows):
    picks, scales = pick_rows(gate_ref[...])
    activ = activate(picks, a_ref, bx_ref, by_ref, g_ref, u_ref, rows)
    for x in range(4):
        dense = gated_blocks(x, picks, scales, activ, d_ref).astype(BF16)
        for yy in range(2):
            out_ref[0, x, yy] = dense[yy * ROWS : (yy + 1) * ROWS, :HALF]
            out_ref[1, x, yy] = dense[yy * ROWS : (yy + 1) * ROWS, HALF:]


def own_up_kernel(a_ref, bx_ref, by_ref, gate_ref, g_ref, u_ref, out_ref, rows):
    picks, _ = pick_rows(gate_ref[...])
    out_ref[...] = activate(picks, a_ref, bx_ref, by_ref, g_ref, u_ref, rows)


def own_down_kernel(activ_ref, gate_ref, d_ref, add_ref, keep_ref, send_ref, both_ref):
    picks, scales = pick_rows(gate_ref[...])
    activ = activ_ref[...]
    for x in range(4):
        dense = gated_blocks(x, picks, scales, activ, d_ref)
        for yy in range(2):
            d = dense[yy * ROWS : (yy + 1) * ROWS]
            part = (d[:, :HALF] + add_ref[0, x, yy].astype(F32)).astype(BF16)
            (send_ref if yy else keep_ref)[x] = part
            both_ref[x, yy] = (d[:, HALF:] + add_ref[1, x, yy].astype(F32)).astype(BF16)


PICKED = SLOTS // 2
ROW_SCRATCH = pltpu.VMEM((PICKED, D), BF16)


def kernel_call(body, out_shape, mib, flops, moved, scratch=()):
    many = isinstance(out_shape, tuple)

    def call(*operands):
        return pl.pallas_call(
            body,
            out_shape=out_shape,
            in_specs=[VM] * len(operands),
            out_specs=(VM,) * len(out_shape) if many else VM,
            scratch_shapes=scratch,
            compiler_params=params(mib),
            cost_estimate=pl.CostEstimate(flops=flops, bytes_accessed=moved, transcendentals=0),
        )(*operands)

    return call


def shape(*dims, dtype=BF16):
    return jax.ShapeDtypeStruct(dims, dtype)


def experts_other(tokens, gates, w_gate, w_up, w_down):
    return kernel_call(
        other_kernel,
        shape(2, 4, 2, ROWS, HALF),
        24,
        6 * PICKED * D * FF,
        16 << 20,
        [ROW_SCRATCH],
    )(*tokens, gates, w_gate, w_up, w_down)


def experts_own_up(tokens, gates, w_gate, w_up):
    return kernel_call(
        own_up_kernel, shape(PICKED, FF), 24, 4 * PICKED * D * FF, 10 << 20, [ROW_SCRATCH]
    )(*tokens, gates, w_gate, w_up)


def experts_own_down(activ, gates, w_down, add):
    return kernel_call(
        own_down_kernel,
        (shape(4, ROWS, HALF), shape(4, ROWS, HALF), shape(4, 2, ROWS, HALF)),
        36,
        2 * PICKED * D * FF,
        12 << 20,
    )(activ, gates, w_down, add)


def final_kernel(hid_ref, x_ref, b_ref, y_ref, out_ref):
    left = hid_ref[:, :HALF]
    for x in range(4):
        left = left + x_ref[x].astype(F32)
    out_ref[:, :HALF] = left.astype(BF16)
    right = hid_ref[:, HALF:] + (b_ref[...] + y_ref[...].astype(F32))
    out_ref[:, HALF:] = right.astype(BF16)


def pass_kernel(in_ref, out_ref):
    out_ref[...] = in_ref[...]


def beside_swap(v):
    return kernel_call(pass_kernel, shape(*v.shape, dtype=F32), 4, 30000000000, 20 << 20)(v)


def spread_tokens(first, second, gates, gates_other, matrices):
    first_y = y_swap(first)
    second_x = x_exchange(second)
    first_y, second_x, gates, gates_other = lax.optimization_barrier(
        (first_y, second_x, gates, gates_other)
    )
    second_y = y_swap(second_x)
    first_all = x_spread(jnp.stack([first, first_y]))
    second_x_other = swap(second_x)
    first_all, second_x_other, gates_other = lax.optimization_barrier(
        (first_all, second_x_other, gates_other)
    )
    gates_other = beside_swap(gates_other)
    own = (first_all, second_x, second_y)
    return own, (swap(first_all), second_x_other, swap(second_y)), gates, gates_other


def reduce_back(keep, send, both, hidden):
    got_y = y_swap(send)
    got_x = x_exchange(both)
    part_a = (keep.astype(F32) + got_y.astype(F32)).astype(BF16)
    part_b = jnp.sum(got_x.astype(F32), axis=0)
    last_y = y_swap(part_b[1].astype(BF16))
    last_x = x_exchange(part_a)
    return kernel_call(final_kernel, shape(ROWS, D), 12, ROWS * D, 4 << 20)(
        hidden, last_x, part_b[0], last_y
    )


def per_device(
    queries,
    keys,
    values,
    segments,
    residual,
    out_weight,
    norm_gain,
    expert_ids,
    gate_weights,
    w_gate,
    w_up,
    w_down,
):
    ctx, exp = lax.axis_index("ctx"), lax.axis_index("exp")
    place = jnp.stack([ctx % Z, ctx // Z, exp // 8, exp % 2]).astype(jnp.int32)
    seg_rows = jnp.broadcast_to(
        jnp.pad(segments.astype(BF16), ((0, 0), (0, 512 - ROWS))), (SEG_ROWS, 512)
    )
    own = jnp.concatenate(
        [jnp.concatenate([keys[0], values[0]], axis=1), seg_rows], axis=0
    )
    upper = lax.ppermute(own, "ctx", [(s, s + Z) for s in range(Z)])
    both_levels = jnp.concatenate([upper, own], axis=0)
    weight, weight_other, both_levels = gather_weight(
        out_weight, gate_rows(expert_ids[0], gate_weights[0]), both_levels
    )
    kv = lax.all_gather(both_levels, "ctx", axis=0, tiled=True, axis_index_groups=Z_GROUPS)
    att = attention(place, queries[0], kv, segments[0].astype(F32)[:, None])
    hidden, first, second = project(att, weight, weight_other, residual[0], norm_gain[None, :])
    matrices = (w_gate[0], w_up[0], w_down[0])
    own, other, gates, gates_other = spread_tokens(
        first, second, own_gates(weight[0], exp), own_gates(weight_other[0], exp), matrices
    )
    partial = swap(experts_other(other, gates_other, *matrices))
    activ = experts_own_up(own, gates, *matrices[:2])
    keep, send, both = experts_own_down(activ, gates, matrices[2], partial)
    return reduce_back(keep, send, both, hidden)[None]


def solution(mesh):
    return jax.shard_map(
        per_device,
        mesh=mesh,
        in_specs=(
            P("exp", "ctx", None),
            P("exp", "ctx", None),
            P("exp", "ctx", None),
            P("exp", "ctx"),
            P("exp", "ctx", None),
            P("exp", None),
            P(),
            P("exp", "ctx", None),
            P("exp", "ctx", None),
            P("exp", None, None),
            P("exp", None, None),
            P("exp", None, None),
        ),
        out_specs=P("exp", "ctx", None),
        check_vma=False,
    )
```

```python
import functools

import jax
import jax.numpy as jnp
from jax import lax
from jax.experimental import pallas as pl
from jax.experimental.pallas import tpu as pltpu
from jax.sharding import PartitionSpec as P

D = 2048
HEADS = 16
HEAD_DIM = 128
ROWS = 128
EXPERTS = 16
CAP = 72
SLOTS = EXPERTS * CAP
FF = 768
HALF = D // 2
Z = 8
SEG_ROWS = 16
PART = ROWS + SEG_ROWS
KEYS = 9 * ROWS
MASKED = -1e30
BF16 = jnp.bfloat16
F32 = jnp.float32

VM = pl.BlockSpec(memory_space=pltpu.VMEM)
SM = pl.BlockSpec(memory_space=pltpu.SMEM)


def params(mib, **kw):
    return pltpu.CompilerParams(vmem_limit_bytes=mib << 20, **kw)


def exp_pairs(f):
    pairs = []
    for e in range(16):
        y, x, c = f(e // 8, (e // 2) % 4, e % 2)
        pairs.append((e, (y % 2) * 8 + (x % 4) * 2 + c % 2))
    return pairs


CORE_SWAP = exp_pairs(lambda y, x, c: (y, x, c + 1))
Y_SWAP = exp_pairs(lambda y, x, c: (y + 1, x, c))
X_GROUPS = [[y * 8 + x * 2 + c for x in range(4)] for y in range(2) for c in range(2)]
Z_GROUPS = [list(range(8)), list(range(8, 16))]


def swap(v):
    return lax.ppermute(v, "exp", CORE_SWAP)


def y_swap(v):
    return lax.ppermute(v, "exp", Y_SWAP)


def x_exchange(v):
    return lax.all_to_all(
        v, "exp", split_axis=0, concat_axis=0, tiled=True, axis_index_groups=X_GROUPS
    )


def x_spread(v):
    return x_exchange(jnp.broadcast_to(v[None], (4,) + v.shape))


def gather_weight(w, extra, after):
    first = jnp.concatenate([w[:, :HALF], extra], axis=0)
    first, after = lax.optimization_barrier((first, after))
    first_y = y_swap(first)
    second_x = x_spread(w[:, HALF:])
    first_y, second_x = lax.optimization_barrier((first_y, second_x))
    second_y = y_swap(second_x)
    first_all = x_spread(jnp.stack([first, first_y]))
    second_x_other = swap(second_x)
    first_all, second_y, second_x_other = lax.optimization_barrier(
        (first_all, second_y, second_x_other)
    )
    own = (first_all, second_x, second_y)
    return own, (swap(first_all), second_x_other, swap(second_y)), after


def gate_rows(ids, gates):
    same = ids[None, :, :] == jnp.arange(EXPERTS, dtype=jnp.int32)[:, None, None]
    table = jnp.sum(jnp.where(same, gates[None], 0.0), axis=2)
    high = table.astype(BF16)
    low = (table - high.astype(F32)).astype(BF16)
    flat = jnp.concatenate([high.reshape(2, HALF), low.reshape(2, HALF)], axis=0)
    return jnp.pad(flat, ((0, 4), (0, 0)))


def own_gates(rows, expert):
    at = (expert % 8) * ROWS
    high = lax.dynamic_slice(rows, (0, 0, ROWS + expert // 8, at), (4, 2, 1, ROWS))
    low = lax.dynamic_slice(rows, (0, 0, ROWS + 2 + expert // 8, at), (4, 2, 1, ROWS))
    return (high.astype(F32) + low.astype(F32)).reshape(8, ROWS)


def attention_kernel(place, q_ref, kv_ref, qseg_ref, out_ref, kcat, bias):
    z, hi, y, c = place[0], place[1], place[2], place[3]
    qpos = (hi * Z + z) * ROWS + lax.broadcasted_iota(jnp.int32, (ROWS, ROWS), 0)
    lane = lax.broadcasted_iota(jnp.int32, (ROWS, ROWS), 1)
    qseg = qseg_ref[...]
    for j in range(9):
        if j < 8:
            upper = (z < j).astype(jnp.int32)
            at = j * (2 * PART) + (1 - upper) * PART
            first = jnp.where(
                upper == 1, jnp.where(hi == 1, j * ROWS, 1 << 20), (hi * Z + j) * ROWS
            )
        else:
            at = z * (2 * PART)
            first = jnp.where(hi == 1, z * ROWS, 1 << 20)
        at = pl.multiple_of(at, 16)
        kcat[pl.ds(j * ROWS, ROWS), :] = kv_ref[pl.ds(at, ROWS), :]
        kseg = kv_ref[pl.ds(pl.multiple_of(at + ROWS, 16), SEG_ROWS), 0:ROWS].astype(F32)[0:1, :]
        visible = (first + lane <= qpos) & (kseg == qseg)
        bias[:, pl.ds(j * ROWS, ROWS)] = jnp.where(visible, F32(0.0), F32(MASKED))
    scale = HEAD_DIM ** (-0.5)
    for rel in range(2):
        for yy in range(2):
            kvh = lax.rem(y + yy, 2)
            base = kvh * 8 + lax.rem(c + rel, 2)
            qs = jnp.concatenate(
                [
                    q_ref[:, pl.ds(pl.multiple_of((base + 2 * x) * HEAD_DIM, 128), HEAD_DIM)]
                    for x in range(4)
                ],
                axis=0,
            )
            k = kcat[:, pl.ds(pl.multiple_of(kvh * HEAD_DIM, 128), HEAD_DIM)]
            v = kcat[:, pl.ds(pl.multiple_of(256 + kvh * HEAD_DIM, 128), HEAD_DIM)]
            s = lax.dot_general(qs, k, (((1,), (1,)), ((), ())), preferred_element_type=F32)
            s = s.reshape(4, ROWS, KEYS) * scale + bias[...][None]
            top = jnp.max(s, axis=-1, keepdims=True)
            w = jnp.exp(s - top)
            total = jnp.sum(w, axis=-1, keepdims=True).reshape(4 * ROWS, 1)
            a = jnp.dot(
                w.astype(BF16).reshape(4 * ROWS, KEYS), v, preferred_element_type=F32
            )
            a = (a / total).astype(BF16)
            for x in range(4):
                out_ref[:, pl.ds(rel * HALF + (2 * x + yy) * HEAD_DIM, HEAD_DIM)] = a[
                    x * ROWS : (x + 1) * ROWS
                ]


def attention(place, q, kv, qseg):
    return pl.pallas_call(
        attention_kernel,
        out_shape=jax.ShapeDtypeStruct((ROWS, D), BF16),
        in_specs=[SM, VM, VM, VM],
        out_specs=VM,
        scratch_shapes=[pltpu.VMEM((KEYS, 512), BF16), pltpu.VMEM((ROWS, KEYS), F32)],
        compiler_params=params(24),
        cost_estimate=pl.CostEstimate(
            flops=4 * HEADS * ROWS * KEYS * HEAD_DIM,
            bytes_accessed=4 << 20,
            transcendentals=HEADS * ROWS * KEYS,
        ),
    )(place, q, kv, qseg)


def right_rows(x_ref, y_ref):
    parts = []
    for x in range(4):
        parts += [x_ref[x], y_ref[x]]
    return jnp.concatenate(parts, axis=0)


def project_kernel(
    att_ref, fo, sox, soy, fx, sxx, sxy, res_ref, gain_ref, hid_ref, first_ref, second_ref
):
    own, other = att_ref[:, :HALF], att_ref[:, HALF:]
    fo_rows = fo[:, :, 0:ROWS, :].reshape(HALF, HALF)
    fx_rows = fx[:, :, 0:ROWS, :].reshape(HALF, HALF)
    left = jnp.dot(own, fo_rows, preferred_element_type=F32) + jnp.dot(
        other, fx_rows, preferred_element_type=F32
    )
    right = jnp.dot(own, right_rows(sox, soy), preferred_element_type=F32) + jnp.dot(
        other, right_rows(sxx, sxy), preferred_element_type=F32
    )
    left = left + res_ref[:, :HALF].astype(F32)
    right = right + res_ref[:, HALF:].astype(F32)
    hid_ref[:, :HALF] = left
    hid_ref[:, HALF:] = right
    square = jnp.sum(left * left, axis=-1, keepdims=True) + jnp.sum(
        right * right, axis=-1, keepdims=True
    )
    scale = lax.rsqrt(square * (1.0 / D) + 1e-06)
    gain = gain_ref[...]
    first_ref[...] = (left * scale * gain[:, :HALF]).astype(BF16)
    second = (right * scale * gain[:, HALF:]).astype(BF16)
    for x in range(4):
        second_ref[x] = second


def project(att, own, other, residual, gain):
    return pl.pallas_call(
        project_kernel,
        out_shape=(
            jax.ShapeDtypeStruct((ROWS, D), F32),
            jax.ShapeDtypeStruct((ROWS, HALF), BF16),
            jax.ShapeDtypeStruct((4, ROWS, HALF), BF16),
        ),
        in_specs=[VM] * 9,
        out_specs=(VM, VM, VM),
        compiler_params=params(50),
        cost_estimate=pl.CostEstimate(
            flops=2 * ROWS * D * D, bytes_accessed=11 << 20, transcendentals=ROWS
        ),
    )(att, *own, *other, residual, gain)


def pick_rows(gates):
    named = (gates > 0.0).astype(F32)
    before = (
        lax.broadcasted_iota(jnp.int32, (ROWS, ROWS), 0)
        < lax.broadcasted_iota(jnp.int32, (ROWS, ROWS), 1)
    ).astype(BF16)
    rank = jnp.dot(named.astype(BF16), before, preferred_element_type=F32)
    rank = jnp.where(named > 0.5, rank, F32(-1.0))
    row = lax.broadcasted_iota(jnp.int32, (2 * CAP, 2 * ROWS), 0)
    lane = lax.broadcasted_iota(jnp.int32, (2 * CAP, 2 * ROWS), 1)
    second = row >= CAP
    slot = jnp.where(second, row - CAP, row)
    slot = jnp.where(second == (lane >= ROWS), slot, -2).astype(F32)
    picks, scales = [], []
    for x in range(4):
        both = jnp.concatenate([rank[2 * x : 2 * x + 1], rank[2 * x + 1 : 2 * x + 2]], axis=1)
        here = (both == slot).astype(F32)
        gate = jnp.concatenate([gates[2 * x : 2 * x + 1], gates[2 * x + 1 : 2 * x + 2]], axis=1)
        scales.append(jnp.sum(here * gate, axis=1, keepdims=True))
        picks.append(here.astype(BF16))
    return picks, scales


def activate(picks, a_ref, bx_ref, by_ref, g_ref, u_ref, rows):
    for x in range(4):
        left = jnp.dot(picks[x], a_ref[x].reshape(2 * ROWS, HALF), preferred_element_type=F32)
        tokens = jnp.concatenate([bx_ref[x], by_ref[x]], axis=0)
        right = jnp.dot(picks[x], tokens, preferred_element_type=F32)
        rows[pl.ds(x * 2 * CAP, 2 * CAP), :HALF] = left.astype(BF16)
        rows[pl.ds(x * 2 * CAP, 2 * CAP), HALF:] = right.astype(BF16)
    gate = jnp.dot(rows[...], g_ref[...], preferred_element_type=F32)
    up = jnp.dot(rows[...], u_ref[...], preferred_element_type=F32)
    return (gate / (1.0 + jnp.exp(-gate)) * up).astype(BF16)


def gated_blocks(x, picks, scales, activ, d_ref):
    o = jnp.dot(activ[x * 2 * CAP : (x + 1) * 2 * CAP], d_ref[...], preferred_element_type=F32)
    o = (o * scales[x]).astype(BF16)
    return lax.dot_general(picks[x], o, (((0,), (0,)), ((), ())), preferred_element_type=F32)


def other_kernel(a_ref, bx_ref, by_ref, gate_ref, g_ref, u_ref, d_ref, out_ref, rows):
    picks, scales = pick_rows(gate_ref[...])
    activ = activate(picks, a_ref, bx_ref, by_ref, g_ref, u_ref, rows)
    for x in range(4):
        dense = gated_blocks(x, picks, scales, activ, d_ref).astype(BF16)
        for yy in range(2):
            out_ref[0, x, yy] = dense[yy * ROWS : (yy + 1) * ROWS, :HALF]
            out_ref[1, x, yy] = dense[yy * ROWS : (yy + 1) * ROWS, HALF:]


def own_up_kernel(a_ref, bx_ref, by_ref, gate_ref, g_ref, u_ref, out_ref, rows):
    picks, _ = pick_rows(gate_ref[...])
    out_ref[...] = activate(picks, a_ref, bx_ref, by_ref, g_ref, u_ref, rows)


def own_down_kernel(activ_ref, gate_ref, d_ref, add_ref, keep_ref, send_ref, both_ref):
    picks, scales = pick_rows(gate_ref[...])
    activ = activ_ref[...]
    for x in range(4):
        dense = gated_blocks(x, picks, scales, activ, d_ref)
        for yy in range(2):
            d = dense[yy * ROWS : (yy + 1) * ROWS]
            part = (d[:, :HALF] + add_ref[0, x, yy].astype(F32)).astype(BF16)
            (send_ref if yy else keep_ref)[x] = part
            both_ref[x, yy] = (d[:, HALF:] + add_ref[1, x, yy].astype(F32)).astype(BF16)


PICKED = SLOTS // 2
ROW_SCRATCH = pltpu.VMEM((PICKED, D), BF16)


def kernel_call(body, out_shape, mib, flops, moved, scratch=()):
    many = isinstance(out_shape, tuple)

    def call(*operands):
        return pl.pallas_call(
            body,
            out_shape=out_shape,
            in_specs=[VM] * len(operands),
            out_specs=(VM,) * len(out_shape) if many else VM,
            scratch_shapes=scratch,
            compiler_params=params(mib),
            cost_estimate=pl.CostEstimate(flops=flops, bytes_accessed=moved, transcendentals=0),
        )(*operands)

    return call


def shape(*dims, dtype=BF16):
    return jax.ShapeDtypeStruct(dims, dtype)


def experts_other(tokens, gates, w_gate, w_up, w_down):
    return kernel_call(
        other_kernel,
        shape(2, 4, 2, ROWS, HALF),
        24,
        6 * PICKED * D * FF,
        16 << 20,
        [ROW_SCRATCH],
    )(*tokens, gates, w_gate, w_up, w_down)


def experts_own_up(tokens, gates, w_gate, w_up):
    return kernel_call(
        own_up_kernel, shape(PICKED, FF), 24, 4 * PICKED * D * FF, 10 << 20, [ROW_SCRATCH]
    )(*tokens, gates, w_gate, w_up)


def experts_own_down(activ, gates, w_down, add):
    return kernel_call(
        own_down_kernel,
        (shape(4, ROWS, HALF), shape(4, ROWS, HALF), shape(4, 2, ROWS, HALF)),
        52,
        2 * PICKED * D * FF,
        12 << 20,
    )(activ, gates, w_down, add)


def final_kernel(hid_ref, x_ref, b_ref, y_ref, out_ref):
    left = hid_ref[:, :HALF]
    for x in range(4):
        left = left + x_ref[x].astype(F32)
    out_ref[:, :HALF] = left.astype(BF16)
    right = hid_ref[:, HALF:] + (b_ref[...] + y_ref[...].astype(F32))
    out_ref[:, HALF:] = right.astype(BF16)


def pass_kernel(in_ref, out_ref):
    out_ref[...] = in_ref[...]


def beside_swap(v):
    return kernel_call(pass_kernel, shape(*v.shape, dtype=F32), 4, 30000000000, 20 << 20)(v)


def spread_tokens(first, second, gates, gates_other, matrices):
    first_y = y_swap(first)
    second_x = x_exchange(second)
    first_y, second_x, gates, gates_other = lax.optimization_barrier(
        (first_y, second_x, gates, gates_other)
    )
    second_y = y_swap(second_x)
    first_all = x_spread(jnp.stack([first, first_y]))
    second_x_other = swap(second_x)
    first_all, second_x_other, gates_other = lax.optimization_barrier(
        (first_all, second_x_other, gates_other)
    )
    gates_other = beside_swap(gates_other)
    own = (first_all, second_x, second_y)
    return own, (swap(first_all), second_x_other, swap(second_y)), gates, gates_other


def reduce_back(keep, send, both, hidden):
    got_y = y_swap(send)
    got_x = x_exchange(both)
    part_a = (keep.astype(F32) + got_y.astype(F32)).astype(BF16)
    part_b = jnp.sum(got_x.astype(F32), axis=0)
    last_y = y_swap(part_b[1].astype(BF16))
    last_x = x_exchange(part_a)
    return kernel_call(final_kernel, shape(ROWS, D), 12, ROWS * D, 4 << 20)(
        hidden, last_x, part_b[0], last_y
    )


def per_device(
    queries,
    keys,
    values,
    segments,
    residual,
    out_weight,
    norm_gain,
    expert_ids,
    gate_weights,
    w_gate,
    w_up,
    w_down,
):
    ctx, exp = lax.axis_index("ctx"), lax.axis_index("exp")
    place = jnp.stack([ctx % Z, ctx // Z, exp // 8, exp % 2]).astype(jnp.int32)
    seg_rows = jnp.broadcast_to(
        jnp.pad(segments.astype(BF16), ((0, 0), (0, 512 - ROWS))), (SEG_ROWS, 512)
    )
    own = jnp.concatenate(
        [jnp.concatenate([keys[0], values[0]], axis=1), seg_rows], axis=0
    )
    upper = lax.ppermute(own, "ctx", [(s, s + Z) for s in range(Z)])
    both_levels = jnp.concatenate([upper, own], axis=0)
    weight, weight_other, both_levels = gather_weight(
        out_weight, gate_rows(expert_ids[0], gate_weights[0]), both_levels
    )
    kv = lax.all_gather(both_levels, "ctx", axis=0, tiled=True, axis_index_groups=Z_GROUPS)
    att = attention(place, queries[0], kv, segments[0].astype(F32)[:, None])
    hidden, first, second = project(att, weight, weight_other, residual[0], norm_gain[None, :])
    matrices = (w_gate[0], w_up[0], w_down[0])
    own, other, gates, gates_other = spread_tokens(
        first, second, own_gates(weight[0], exp), own_gates(weight_other[0], exp), matrices
    )
    partial = swap(experts_other(other, gates_other, *matrices))
    activ = experts_own_up(own, gates, *matrices[:2])
    keep, send, both = experts_own_down(activ, gates, matrices[2], partial)
    return reduce_back(keep, send, both, hidden)[None]


def solution(mesh):
    return jax.shard_map(
        per_device,
        mesh=mesh,
        in_specs=(
            P("exp", "ctx", None),
            P("exp", "ctx", None),
            P("exp", "ctx", None),
            P("exp", "ctx"),
            P("exp", "ctx", None),
            P("exp", None),
            P(),
            P("exp", "ctx", None),
            P("exp", "ctx", None),
            P("exp", None, None),
            P("exp", None, None),
            P("exp", None, None),
        ),
        out_specs=P("exp", "ctx", None),
        check_vma=False,
    )
```

```python
import functools

import jax
import jax.numpy as jnp
from jax import lax
from jax.experimental import pallas as pl
from jax.experimental.pallas import tpu as pltpu
from jax.sharding import PartitionSpec as P

D = 2048
HEADS = 16
HEAD_DIM = 128
ROWS = 128
EXPERTS = 16
CAP = 72
SLOTS = EXPERTS * CAP
FF = 768
HALF = D // 2
Z = 8
SEG_ROWS = 16
PART = ROWS + SEG_ROWS
KEYS = 9 * ROWS
MASKED = -1e30
LOG2_E = 1.4426950408889634
BF16 = jnp.bfloat16
F32 = jnp.float32

VM = pl.BlockSpec(memory_space=pltpu.VMEM)
SM = pl.BlockSpec(memory_space=pltpu.SMEM)


def params(mib, **kw):
    return pltpu.CompilerParams(vmem_limit_bytes=mib << 20, **kw)


def exp_pairs(f):
    pairs = []
    for e in range(16):
        y, x, c = f(e // 8, (e // 2) % 4, e % 2)
        pairs.append((e, (y % 2) * 8 + (x % 4) * 2 + c % 2))
    return pairs


CORE_SWAP = exp_pairs(lambda y, x, c: (y, x, c + 1))
Y_SWAP = exp_pairs(lambda y, x, c: (y + 1, x, c))
X_GROUPS = [[y * 8 + x * 2 + c for x in range(4)] for y in range(2) for c in range(2)]
Z_GROUPS = [list(range(8)), list(range(8, 16))]


def swap(v):
    return lax.ppermute(v, "exp", CORE_SWAP)


def y_swap(v):
    return lax.ppermute(v, "exp", Y_SWAP)


def x_exchange(v):
    return lax.all_to_all(
        v, "exp", split_axis=0, concat_axis=0, tiled=True, axis_index_groups=X_GROUPS
    )


def x_spread(v):
    return x_exchange(jnp.broadcast_to(v[None], (4,) + v.shape))


def gather_weight(w, extra, after):
    first = jnp.concatenate([w[:, :HALF], extra], axis=0)
    first, after = lax.optimization_barrier((first, after))
    first_y = y_swap(first)
    second_x = x_spread(w[:, HALF:])
    first_y, second_x = lax.optimization_barrier((first_y, second_x))
    second_y = y_swap(second_x)
    first_all = x_spread(jnp.stack([first, first_y]))
    second_x_other = swap(second_x)
    first_all, second_y, second_x_other = lax.optimization_barrier(
        (first_all, second_y, second_x_other)
    )
    own = (first_all, second_x, second_y)
    return own, (swap(first_all), second_x_other, swap(second_y)), after


def gate_rows(ids, gates):
    same = ids[None, :, :] == jnp.arange(EXPERTS, dtype=jnp.int32)[:, None, None]
    table = jnp.sum(jnp.where(same, gates[None], 0.0), axis=2)
    high = table.astype(BF16)
    low = (table - high.astype(F32)).astype(BF16)
    flat = jnp.concatenate([high.reshape(2, HALF), low.reshape(2, HALF)], axis=0)
    return jnp.pad(flat, ((0, 4), (0, 0)))


def own_gates(rows, expert):
    at = (expert % 8) * ROWS
    high = lax.dynamic_slice(rows, (0, 0, ROWS + expert // 8, at), (4, 2, 1, ROWS))
    low = lax.dynamic_slice(rows, (0, 0, ROWS + 2 + expert // 8, at), (4, 2, 1, ROWS))
    return (high.astype(F32) + low.astype(F32)).reshape(8, ROWS)


def attention_kernel(place, q_ref, kv_ref, qseg_ref, out_ref, kcat, bias):
    z, hi, y, c = place[0], place[1], place[2], place[3]
    qpos = (hi * Z + z) * ROWS + lax.broadcasted_iota(jnp.int32, (ROWS, ROWS), 0)
    lane = lax.broadcasted_iota(jnp.int32, (ROWS, ROWS), 1)
    qseg = qseg_ref[...]
    for j in range(9):
        if j < 8:
            upper = (z < j).astype(jnp.int32)
            at = j * (2 * PART) + (1 - upper) * PART
            first = jnp.where(
                upper == 1, jnp.where(hi == 1, j * ROWS, 1 << 20), (hi * Z + j) * ROWS
            )
        else:
            at = z * (2 * PART)
            first = jnp.where(hi == 1, z * ROWS, 1 << 20)
        at = pl.multiple_of(at, 16)
        kcat[pl.ds(j * ROWS, ROWS), :] = kv_ref[pl.ds(at, ROWS), :]
        kseg = kv_ref[pl.ds(pl.multiple_of(at + ROWS, 16), SEG_ROWS), 0:ROWS].astype(F32)[0:1, :]
        visible = (first + lane <= qpos) & (kseg == qseg)
        bias[:, pl.ds(j * ROWS, ROWS)] = jnp.where(visible, F32(0.0), F32(MASKED))
    scale = HEAD_DIM ** (-0.5) * LOG2_E
    for rel in range(2):
        for yy in range(2):
            kvh = lax.rem(y + yy, 2)
            base = kvh * 8 + lax.rem(c + rel, 2)
            qs = jnp.concatenate(
                [
                    q_ref[:, pl.ds(pl.multiple_of((base + 2 * x) * HEAD_DIM, 128), HEAD_DIM)]
                    for x in range(4)
                ],
                axis=0,
            )
            k = kcat[:, pl.ds(pl.multiple_of(kvh * HEAD_DIM, 128), HEAD_DIM)]
            v = kcat[:, pl.ds(pl.multiple_of(256 + kvh * HEAD_DIM, 128), HEAD_DIM)]
            s = lax.dot_general(qs, k, (((1,), (1,)), ((), ())), preferred_element_type=F32)
            s = s.reshape(4, ROWS, KEYS) * scale + bias[...][None]
            top = jnp.max(s, axis=-1, keepdims=True)
            w = jnp.exp2(s - top)
            total = jnp.sum(w, axis=-1, keepdims=True).reshape(4 * ROWS, 1)
            a = jnp.dot(
                w.astype(BF16).reshape(4 * ROWS, KEYS), v, preferred_element_type=F32
            )
            a = (a / total).astype(BF16)
            for x in range(4):
                out_ref[:, pl.ds(rel * HALF + (2 * x + yy) * HEAD_DIM, HEAD_DIM)] = a[
                    x * ROWS : (x + 1) * ROWS
                ]


def attention(place, q, kv, qseg):
    return pl.pallas_call(
        attention_kernel,
        out_shape=jax.ShapeDtypeStruct((ROWS, D), BF16),
        in_specs=[SM, VM, VM, VM],
        out_specs=VM,
        scratch_shapes=[pltpu.VMEM((KEYS, 512), BF16), pltpu.VMEM((ROWS, KEYS), F32)],
        compiler_params=params(24),
        cost_estimate=pl.CostEstimate(
            flops=4 * HEADS * ROWS * KEYS * HEAD_DIM,
            bytes_accessed=4 << 20,
            transcendentals=HEADS * ROWS * KEYS,
        ),
    )(place, q, kv, qseg)


def right_rows(x_ref, y_ref):
    parts = []
    for x in range(4):
        parts += [x_ref[x], y_ref[x]]
    return jnp.concatenate(parts, axis=0)


def project_kernel(
    att_ref, fo, sox, soy, fx, sxx, sxy, res_ref, gain_ref, hid_ref, first_ref, second_ref
):
    own, other = att_ref[:, :HALF], att_ref[:, HALF:]
    fo_rows = fo[:, :, 0:ROWS, :].reshape(HALF, HALF)
    fx_rows = fx[:, :, 0:ROWS, :].reshape(HALF, HALF)
    left = jnp.dot(own, fo_rows, preferred_element_type=F32) + jnp.dot(
        other, fx_rows, preferred_element_type=F32
    )
    right = jnp.dot(own, right_rows(sox, soy), preferred_element_type=F32) + jnp.dot(
        other, right_rows(sxx, sxy), preferred_element_type=F32
    )
    left = left + res_ref[:, :HALF].astype(F32)
    right = right + res_ref[:, HALF:].astype(F32)
    hid_ref[:, :HALF] = left
    hid_ref[:, HALF:] = right
    square = jnp.sum(left * left, axis=-1, keepdims=True) + jnp.sum(
        right * right, axis=-1, keepdims=True
    )
    scale = lax.rsqrt(square * (1.0 / D) + 1e-06)
    gain = gain_ref[...]
    first_ref[...] = (left * scale * gain[:, :HALF]).astype(BF16)
    second = (right * scale * gain[:, HALF:]).astype(BF16)
    for x in range(4):
        second_ref[x] = second


def project(att, own, other, residual, gain):
    return pl.pallas_call(
        project_kernel,
        out_shape=(
            jax.ShapeDtypeStruct((ROWS, D), F32),
            jax.ShapeDtypeStruct((ROWS, HALF), BF16),
            jax.ShapeDtypeStruct((4, ROWS, HALF), BF16),
        ),
        in_specs=[VM] * 9,
        out_specs=(VM, VM, VM),
        compiler_params=params(50),
        cost_estimate=pl.CostEstimate(
            flops=2 * ROWS * D * D, bytes_accessed=11 << 20, transcendentals=ROWS
        ),
    )(att, *own, *other, residual, gain)


def pick_rows(gates):
    named = (gates > 0.0).astype(F32)
    before = (
        lax.broadcasted_iota(jnp.int32, (ROWS, ROWS), 0)
        < lax.broadcasted_iota(jnp.int32, (ROWS, ROWS), 1)
    ).astype(BF16)
    rank = jnp.dot(named.astype(BF16), before, preferred_element_type=F32)
    rank = jnp.where(named > 0.5, rank, F32(-1.0))
    row = lax.broadcasted_iota(jnp.int32, (2 * CAP, 2 * ROWS), 0)
    lane = lax.broadcasted_iota(jnp.int32, (2 * CAP, 2 * ROWS), 1)
    second = row >= CAP
    slot = jnp.where(second, row - CAP, row)
    slot = jnp.where(second == (lane >= ROWS), slot, -2).astype(F32)
    picks, scales = [], []
    for x in range(4):
        both = jnp.concatenate([rank[2 * x : 2 * x + 1], rank[2 * x + 1 : 2 * x + 2]], axis=1)
        here = (both == slot).astype(F32)
        gate = jnp.concatenate([gates[2 * x : 2 * x + 1], gates[2 * x + 1 : 2 * x + 2]], axis=1)
        scales.append(jnp.sum(here * gate, axis=1, keepdims=True))
        picks.append(here.astype(BF16))
    return picks, scales


def activate(picks, a_ref, bx_ref, by_ref, g_ref, u_ref, rows):
    for x in range(4):
        left = jnp.dot(picks[x], a_ref[x].reshape(2 * ROWS, HALF), preferred_element_type=F32)
        tokens = jnp.concatenate([bx_ref[x], by_ref[x]], axis=0)
        right = jnp.dot(picks[x], tokens, preferred_element_type=F32)
        rows[pl.ds(x * 2 * CAP, 2 * CAP), :HALF] = left.astype(BF16)
        rows[pl.ds(x * 2 * CAP, 2 * CAP), HALF:] = right.astype(BF16)
    gate = jnp.dot(rows[...], g_ref[...], preferred_element_type=F32)
    up = jnp.dot(rows[...], u_ref[...], preferred_element_type=F32)
    return (gate / (1.0 + jnp.exp(-gate)) * up).astype(BF16)


def gated_blocks(x, picks, scales, activ, d_ref):
    o = jnp.dot(activ[x * 2 * CAP : (x + 1) * 2 * CAP], d_ref[...], preferred_element_type=F32)
    o = (o * scales[x]).astype(BF16)
    return lax.dot_general(picks[x], o, (((0,), (0,)), ((), ())), preferred_element_type=F32)


def other_kernel(a_ref, bx_ref, by_ref, gate_ref, g_ref, u_ref, d_ref, out_ref, rows):
    picks, scales = pick_rows(gate_ref[...])
    activ = activate(picks, a_ref, bx_ref, by_ref, g_ref, u_ref, rows)
    for x in range(4):
        dense = gated_blocks(x, picks, scales, activ, d_ref).astype(BF16)
        for yy in range(2):
            out_ref[0, x, yy] = dense[yy * ROWS : (yy + 1) * ROWS, :HALF]
            out_ref[1, x, yy] = dense[yy * ROWS : (yy + 1) * ROWS, HALF:]


def own_up_kernel(a_ref, bx_ref, by_ref, gate_ref, g_ref, u_ref, out_ref, rows):
    picks, _ = pick_rows(gate_ref[...])
    out_ref[...] = activate(picks, a_ref, bx_ref, by_ref, g_ref, u_ref, rows)


def own_down_kernel(activ_ref, gate_ref, d_ref, add_ref, keep_ref, send_ref, both_ref):
    picks, scales = pick_rows(gate_ref[...])
    activ = activ_ref[...]
    for x in range(4):
        dense = gated_blocks(x, picks, scales, activ, d_ref)
        for yy in range(2):
            d = dense[yy * ROWS : (yy + 1) * ROWS]
            part = (d[:, :HALF] + add_ref[0, x, yy].astype(F32)).astype(BF16)
            (send_ref if yy else keep_ref)[x] = part
            both_ref[x, yy] = (d[:, HALF:] + add_ref[1, x, yy].astype(F32)).astype(BF16)


PICKED = SLOTS // 2
ROW_SCRATCH = pltpu.VMEM((PICKED, D), BF16)


def kernel_call(body, out_shape, mib, flops, moved, scratch=()):
    many = isinstance(out_shape, tuple)

    def call(*operands):
        return pl.pallas_call(
            body,
            out_shape=out_shape,
            in_specs=[VM] * len(operands),
            out_specs=(VM,) * len(out_shape) if many else VM,
            scratch_shapes=scratch,
            compiler_params=params(mib),
            cost_estimate=pl.CostEstimate(flops=flops, bytes_accessed=moved, transcendentals=0),
        )(*operands)

    return call


def shape(*dims, dtype=BF16):
    return jax.ShapeDtypeStruct(dims, dtype)


def experts_other(tokens, gates, w_gate, w_up, w_down):
    return kernel_call(
        other_kernel,
        shape(2, 4, 2, ROWS, HALF),
        24,
        6 * PICKED * D * FF,
        16 << 20,
        [ROW_SCRATCH],
    )(*tokens, gates, w_gate, w_up, w_down)


def experts_own_up(tokens, gates, w_gate, w_up):
    return kernel_call(
        own_up_kernel, shape(PICKED, FF), 24, 4 * PICKED * D * FF, 10 << 20, [ROW_SCRATCH]
    )(*tokens, gates, w_gate, w_up)


def experts_own_down(activ, gates, w_down, add):
    return kernel_call(
        own_down_kernel,
        (shape(4, ROWS, HALF), shape(4, ROWS, HALF), shape(4, 2, ROWS, HALF)),
        36,
        2 * PICKED * D * FF,
        12 << 20,
    )(activ, gates, w_down, add)


def final_kernel(hid_ref, x_ref, b_ref, y_ref, out_ref):
    left = hid_ref[:, :HALF]
    for x in range(4):
        left = left + x_ref[x].astype(F32)
    out_ref[:, :HALF] = left.astype(BF16)
    right = hid_ref[:, HALF:] + (b_ref[...] + y_ref[...].astype(F32))
    out_ref[:, HALF:] = right.astype(BF16)


def pass_kernel(in_ref, out_ref):
    out_ref[...] = in_ref[...]


def beside_swap(v):
    return kernel_call(pass_kernel, shape(*v.shape, dtype=F32), 4, 30000000000, 20 << 20)(v)


def spread_tokens(first, second, gates, gates_other, matrices):
    first_y = y_swap(first)
    second_x = x_exchange(second)
    first_y, second_x, gates, gates_other = lax.optimization_barrier(
        (first_y, second_x, gates, gates_other)
    )
    second_y = y_swap(second_x)
    first_all = x_spread(jnp.stack([first, first_y]))
    second_x_other = swap(second_x)
    first_all, second_x_other, gates_other = lax.optimization_barrier(
        (first_all, second_x_other, gates_other)
    )
    gates_other = beside_swap(gates_other)
    own = (first_all, second_x, second_y)
    return own, (swap(first_all), second_x_other, swap(second_y)), gates, gates_other


def reduce_back(keep, send, both, hidden):
    got_y = y_swap(send)
    got_x = x_exchange(both)
    part_a = (keep.astype(F32) + got_y.astype(F32)).astype(BF16)
    part_b = jnp.sum(got_x.astype(F32), axis=0)
    last_y = y_swap(part_b[1].astype(BF16))
    last_x = x_exchange(part_a)
    return kernel_call(final_kernel, shape(ROWS, D), 12, ROWS * D, 4 << 20)(
        hidden, last_x, part_b[0], last_y
    )


def per_device(
    queries,
    keys,
    values,
    segments,
    residual,
    out_weight,
    norm_gain,
    expert_ids,
    gate_weights,
    w_gate,
    w_up,
    w_down,
):
    ctx, exp = lax.axis_index("ctx"), lax.axis_index("exp")
    place = jnp.stack([ctx % Z, ctx // Z, exp // 8, exp % 2]).astype(jnp.int32)
    seg_rows = jnp.broadcast_to(
        jnp.pad(segments.astype(BF16), ((0, 0), (0, 512 - ROWS))), (SEG_ROWS, 512)
    )
    own = jnp.concatenate(
        [jnp.concatenate([keys[0], values[0]], axis=1), seg_rows], axis=0
    )
    upper = lax.ppermute(own, "ctx", [(s, s + Z) for s in range(Z)])
    both_levels = jnp.concatenate([upper, own], axis=0)
    weight, weight_other, both_levels = gather_weight(
        out_weight, gate_rows(expert_ids[0], gate_weights[0]), both_levels
    )
    kv = lax.all_gather(both_levels, "ctx", axis=0, tiled=True, axis_index_groups=Z_GROUPS)
    att = attention(place, queries[0], kv, segments[0].astype(F32)[:, None])
    hidden, first, second = project(att, weight, weight_other, residual[0], norm_gain[None, :])
    matrices = (w_gate[0], w_up[0], w_down[0])
    own, other, gates, gates_other = spread_tokens(
        first, second, own_gates(weight[0], exp), own_gates(weight_other[0], exp), matrices
    )
    partial = swap(experts_other(other, gates_other, *matrices))
    activ = experts_own_up(own, gates, *matrices[:2])
    keep, send, both = experts_own_down(activ, gates, matrices[2], partial)
    return reduce_back(keep, send, both, hidden)[None]


def solution(mesh):
    return jax.shard_map(
        per_device,
        mesh=mesh,
        in_specs=(
            P("exp", "ctx", None),
            P("exp", "ctx", None),
            P("exp", "ctx", None),
            P("exp", "ctx"),
            P("exp", "ctx", None),
            P("exp", None),
            P(),
            P("exp", "ctx", None),
            P("exp", "ctx", None),
            P("exp", None, None),
            P("exp", None, None),
            P("exp", None, None),
        ),
        out_specs=P("exp", "ctx", None),
        check_vma=False,
    )
```
